512 devices in a mesh: row: 16 (over z), col: 32 (over x, y, core).
Axes of the slice: x: 4, y: 4, z: 16, core: 2. Of those that a mesh axis runs over, the one named last changes fastest.
Arguments:
- matrix: float32 [16384, 16384], P('row', 'col'), as said below
Outputs:
- factored: float32 [16384, 16384], P('row', 'col')
Inputs may be any that keep to these rules, and one draw needn't show every extreme that they name: matrix in natural order is symmetric positive definite.
All inputs are finite; a program needn't handle non-finite values.
Results may differ from the reference program's by a relative error of at most 0.0003.
Values sent between devices are 32-bit elements; how exact they have to be, the bound alone decides.
No kernel may reach another device: no remote copies, remote signals or barrier semaphores. Data moves between devices by JAX's collectives and lax.ppermute only.
A program may use at most 64 MiB of HBM per device.

```python
import math
import jax
import jax.numpy as jnp
from jax import lax

TILE = 128
TR_DEV = 8
PANELS = 2
TC_DEV = 4
ORDER = 16384
N_ROW = 16
N_COL = 32


def draw_matrix(key, part):
    key_feat, key_scale, key_ridge, key_shared = jax.random.split(key, 4)
    features_dim = 1024
    weight_total = sum((1.0 / (1.0 + j) for j in range(features_dim)))
    weights = 1.0 / (1.0 + jnp.arange(features_dim, dtype=jnp.float32))
    column_scales = jnp.sqrt(weights / weight_total)
    raw_features = jax.random.normal(key_feat, (ORDER, features_dim), jnp.float32)
    features = raw_features * column_scales[None, :]
    row_scales = jnp.exp(jax.random.uniform(key_scale, (ORDER,), jnp.float32, math.log(0.5), math.log(2.0)))
    features = features * row_scales[:, None]
    natural = jnp.dot(features, features.T, precision=lax.Precision.HIGHEST, preferred_element_type=jnp.float32)
    ridge_terms = jax.random.uniform(key_ridge, (ORDER,), jnp.float32, 0.5, 1.5)
    diag_index = jnp.arange(ORDER, dtype=jnp.int32)
    natural = natural.at[diag_index, diag_index].add(ridge_terms)
    by_rows = natural.reshape(TR_DEV, N_ROW, TILE, ORDER).transpose(1, 0, 2, 3).reshape(ORDER, ORDER)
    return by_rows.reshape(ORDER, TC_DEV, N_COL, TILE).transpose(0, 2, 1, 3).reshape(ORDER, ORDER)


def setup_inputs(seed: int = 0) -> dict:
    arg_keys = jax.random.split(jax.random.key(seed), 2)
    matrix = draw_matrix(jax.random.fold_in(arg_keys[1], 71), 0)
    return dict(matrix=matrix)


def unpermute(stored):
    order = stored.shape[0]
    rows_local = order // (N_ROW * TILE)
    cols_local = order // (N_COL * TILE)
    by_rows = stored.reshape(N_ROW, rows_local, TILE, order).transpose(1, 0, 2, 3).reshape(order, order)
    return by_rows.reshape(order, N_COL, cols_local, TILE).transpose(0, 2, 1, 3).reshape(order, order)

def permute(natural):
    order = natural.shape[0]
    rows_local = order // (N_ROW * TILE)
    cols_local = order // (N_COL * TILE)
    by_rows = natural.reshape(rows_local, N_ROW, TILE, order).transpose(1, 0, 2, 3).reshape(order, order)
    return by_rows.reshape(order, cols_local, N_COL, TILE).transpose(0, 2, 1, 3).reshape(order, order)

def reference(matrix):
    gauss = unpermute(matrix)
    order = gauss.shape[0]
    for panel_index in range(PANELS):
        start = panel_index * TILE
        stop = start + TILE
        factor = jnp.linalg.cholesky(gauss[start:stop, start:stop])
        below = gauss[stop:, start:stop]
        panel_rows = jax.scipy.linalg.solve_triangular(factor, below.T, lower=True).T
        trailing = gauss[stop:, stop:] - jnp.dot(panel_rows, panel_rows.T, precision=lax.Precision.HIGHEST)
        gauss = gauss.at[stop:, stop:].set(trailing)
        gauss = gauss.at[start:stop, start:stop].set(factor)
        gauss = gauss.at[stop:, start:stop].set(panel_rows)
    tiles = jnp.arange(order) // TILE
    gauss = jnp.where(tiles[:, None] < tiles[None, :], jnp.float32(0.0), gauss)
    return permute(gauss)
```

```python
import jax
import jax.numpy as jnp
from jax import lax
from jax.experimental import pallas as pl
from jax.experimental.pallas import tpu as pltpu
from jax.sharding import PartitionSpec as P

TILE = 128
PANELS = 2
WIDTH = TILE * PANELS
STRIP = 32
GROUP = 8
HIGHEST = lax.Precision.HIGHEST


def product(lhs, rhs, contract):
    return lax.dot_general(
        lhs, rhs, (contract, ((), ())), precision=HIGHEST, preferred_element_type=jnp.float32
    )


def eliminate(strip, pivot_lane):
    tiles = [strip[t * GROUP : (t + 1) * GROUP] for t in range(STRIP // GROUP)]
    sub_row = lax.broadcasted_iota(jnp.int32, (GROUP, 1), 0)
    scales = [jnp.ones((GROUP, 1), jnp.float32) for _ in tiles]
    for i in range(STRIP):
        lane = pivot_lane + i
        own, sub = divmod(i, GROUP)
        row = tiles[own][sub : sub + 1, :]
        pivot = tiles[own][sub : sub + 1, lane : lane + 1]
        inverse = 1.0 / pivot
        scales[own] = jnp.where(sub_row == sub, lax.rsqrt(pivot), scales[own])
        for t in range(own, STRIP // GROUP):
            factor = tiles[t][:, lane : lane + 1] * inverse
            if t == own:
                factor = jnp.where(sub_row > sub, factor, 0.0)
            tiles[t] = tiles[t] - factor * row
    return jnp.concatenate([tile * scale for tile, scale in zip(tiles, scales)], axis=0)


def inverse_factor_kernel(diag_ref, inverse_ref, work_ref):
    for p in range(PANELS):
        rows = slice(p * TILE, (p + 1) * TILE)
        work_ref[rows, :] = diag_ref[: TILE // GROUP, p].reshape(TILE, WIDTH)
    at_row = lax.broadcasted_iota(jnp.int32, (WIDTH, WIDTH), 0)
    at_col = lax.broadcasted_iota(jnp.int32, (WIDTH, WIDTH), 1)
    inverse_ref[...] = jnp.where(at_row == at_col, 1.0, 0.0).astype(jnp.float32)
    for start in range(0, WIDTH, STRIP):
        stop = start + STRIP
        first = start // TILE * TILE
        upper = WIDTH - first
        done = first + TILE
        strip = jnp.concatenate(
            [work_ref[start:stop, first:], inverse_ref[start:stop, :done]], axis=1
        )
        strip = eliminate(strip, start - first)
        inverse_ref[start:stop, :done] = strip[:, upper:]
        if stop < WIDTH:
            update = product(strip[:, :upper], strip, ((0,), (0,)))[stop - first :]
            work_ref[stop:, first:] = work_ref[stop:, first:] - update[:, :upper]
            inverse_ref[stop:, :done] = inverse_ref[stop:, :done] - update[:, upper:]


def inverse_factor(diag):
    return pl.pallas_call(
        inverse_factor_kernel,
        out_shape=jax.ShapeDtypeStruct((WIDTH, WIDTH), jnp.float32),
        scratch_shapes=[pltpu.VMEM((WIDTH, WIDTH), jnp.float32)],
        name="inverse_factor",
    )(diag)


def trailing_kernel(place_ref, matrix_ref, rows_ref, cols_ref, inverse_ref, out_ref, solved_ref):
    step = pl.program_id(0)
    grid_rows, grid_cols, row_index, col_index = (place_ref[k] for k in range(4))
    inverse = inverse_ref[...]
    tile_cols = matrix_ref.shape[1] // TILE

    @pl.when(step == 0)
    def _():
        cols = jnp.concatenate(
            [cols_ref[:, p].reshape(TILE, matrix_ref.shape[1]) for p in range(PANELS)], axis=0
        )
        solved_ref[...] = product(inverse, cols, ((1,), (0,)))

    raw = jnp.concatenate(
        [rows_ref[:, p, 0].reshape(TILE, TILE) for p in range(PANELS)], axis=1
    )
    lower = product(raw, inverse, ((1,), (1,)))
    trailing = matrix_ref[...] - product(lower, solved_ref[...], ((1,), (0,)))
    tile_row = step * grid_rows + row_index
    at_row = lax.broadcasted_iota(jnp.int32, (TILE, TILE), 0)
    at_col = lax.broadcasted_iota(jnp.int32, (TILE, TILE), 1)
    for b in range(tile_cols):
        span = slice(b * TILE, (b + 1) * TILE)
        tile_col = b * grid_cols + col_index
        value = trailing[:, span]
        for p in range(PANELS):
            value = jnp.where(tile_col == p, lower[:, p * TILE : (p + 1) * TILE], value)
        keep = (tile_row - tile_col) * TILE + at_row - at_col >= 0
        keep = keep | ((tile_row == tile_col) & (tile_col >= PANELS))
        out_ref[:, span] = jnp.where(keep, value, 0.0)


def trailing(place, matrix, rows, cols, inverse):
    rows_count, cols_count = matrix.shape
    peers, _, groups, _, _ = rows.shape
    parts = rows_count // TILE // groups
    return pl.pallas_call(
        trailing_kernel,
        grid=(rows_count // TILE,),
        out_shape=jax.ShapeDtypeStruct(matrix.shape, jnp.float32),
        in_specs=[
            pl.BlockSpec(memory_space=pltpu.SMEM),
            pl.BlockSpec((TILE, cols_count), lambda t: (t, 0)),
            pl.BlockSpec(
                (peers // parts, PANELS, 1, GROUP, TILE), lambda t: (t % parts, 0, t // parts, 0, 0)
            ),
            pl.BlockSpec(cols.shape, lambda t: (0, 0, 0, 0)),
            pl.BlockSpec(inverse.shape, lambda t: (0, 0)),
        ],
        out_specs=pl.BlockSpec((TILE, cols_count), lambda t: (t, 0)),
        scratch_shapes=[pltpu.VMEM((WIDTH, cols_count), jnp.float32)],
        name="trailing",
    )(place, matrix, rows, cols, inverse)


def exchange(chunks, axis):
    return lax.all_to_all(chunks, axis, 0, 0, tiled=True)


def to_all(part, axis):
    count = lax.axis_size(axis)
    return exchange(jnp.broadcast_to(part[None], (count, *part.shape)), axis)


def on_device(matrix):
    rows_count, cols_count = matrix.shape
    grid_rows = lax.axis_size("row")
    grid_cols = lax.axis_size("col")
    groups = rows_count // (grid_cols * GROUP)
    with jax.named_scope("scatter_rows"):
        panel = matrix[:, :TILE].reshape(groups, grid_cols, GROUP, TILE).transpose(1, 0, 2, 3)
        row_part = exchange(panel, "col")[:PANELS]
    with jax.named_scope("scatter_cols"):
        col_part = exchange(matrix[:TILE].reshape(grid_rows, GROUP, cols_count), "row")[:PANELS]
    with jax.named_scope("spread_diagonal"):
        own_diag = row_part[:, 0].transpose(1, 0, 2).reshape(GROUP, PANELS * TILE)
        diag_part = to_all(own_diag, "row")[:PANELS]
        diag = to_all(diag_part, "col")
    with jax.named_scope("gather_rows"):
        rows = to_all(row_part, "col")
    with jax.named_scope("gather_cols"):
        cols = to_all(col_part, "row")
    inverse = inverse_factor(diag)
    place = jnp.stack(
        [jnp.int32(grid_rows), jnp.int32(grid_cols), lax.axis_index("row"), lax.axis_index("col")]
    ).astype(jnp.int32)
    return trailing(place, matrix, rows, cols, inverse)


def solution(mesh):
    return jax.shard_map(
        on_device, mesh=mesh, in_specs=(P("row", "col"),), out_specs=P("row", "col"), check_vma=False
    )
```

```python
import jax
import jax.numpy as jnp
from jax import lax
from jax.experimental import pallas as pl
from jax.experimental.pallas import tpu as pltpu
from jax.sharding import PartitionSpec as P

TILE = 128
PANELS = 2
WIDTH = TILE * PANELS
STRIP = 64
GROUP = 8
HIGHEST = lax.Precision.HIGHEST


def product(lhs, rhs, contract):
    return lax.dot_general(
        lhs, rhs, (contract, ((), ())), precision=HIGHEST, preferred_element_type=jnp.float32
    )


def split(value):
    high = value.astype(jnp.bfloat16)
    return high, (value - high.astype(jnp.float32)).astype(jnp.bfloat16)


def eliminate(strip, pivot_lane):
    count, width = strip.shape
    tiles = [
        [strip[t * GROUP : (t + 1) * GROUP, v * TILE : (v + 1) * TILE] for v in range(width // TILE)]
        for t in range(count // GROUP)
    ]
    shape = (GROUP, TILE)
    sub_row = lax.broadcasted_iota(jnp.int32, shape, 0)
    pivots = [jnp.ones(shape, jnp.float32) for _ in tiles]
    for i in range(count):
        block, lane = divmod(pivot_lane + i, TILE)
        own, sub = divmod(i, GROUP)
        below = range(own, count // GROUP)
        columns = [jnp.broadcast_to(tiles[t][block][:, lane : lane + 1], shape) for t in below]
        pivot = jnp.broadcast_to(columns[0][sub : sub + 1], shape)
        pivots[own] = jnp.where(sub_row == sub, pivot, pivots[own])
        inverse = 1.0 / pivot
        rows = [jnp.broadcast_to(part[sub : sub + 1], shape) * inverse for part in tiles[own]]
        columns[0] = jnp.where(sub_row > sub, columns[0], 0.0)
        for t, column in zip(below, columns):
            tiles[t] = [part - column * row for part, row in zip(tiles[t], rows)]
    scaled = []
    for parts, pivot in zip(tiles, pivots):
        scale = lax.rsqrt(pivot)
        scaled.append(jnp.concatenate([part * scale for part in parts], axis=1))
    return jnp.concatenate(scaled, axis=0)


def inverse_factor_kernel(diag_ref, inverse_ref, work_ref):
    for p in range(PANELS):
        rows = slice(p * TILE, (p + 1) * TILE)
        work_ref[rows, :] = diag_ref[:, p].reshape(TILE, WIDTH)
    at_row = lax.broadcasted_iota(jnp.int32, (WIDTH, WIDTH), 0)
    at_col = lax.broadcasted_iota(jnp.int32, (WIDTH, WIDTH), 1)
    inverse_ref[...] = jnp.where(at_row == at_col, 1.0, 0.0).astype(jnp.float32)
    for start in range(0, WIDTH, STRIP):
        stop = start + STRIP
        first = start // TILE * TILE
        upper = WIDTH - first
        done = first + TILE
        strip = jnp.concatenate(
            [work_ref[start:stop, first:], inverse_ref[start:stop, :done]], axis=1
        )
        strip = eliminate(strip, start - first)
        inverse_ref[start:stop, :done] = strip[:, upper:]
        if stop < WIDTH:
            update = product(strip[:, :upper], strip, ((0,), (0,)))[stop - first :]
            work_ref[stop:, first:] = work_ref[stop:, first:] - update[:, :upper]
            inverse_ref[stop:, :done] = inverse_ref[stop:, :done] - update[:, upper:]


def inverse_factor(diag):
    return pl.pallas_call(
        inverse_factor_kernel,
        grid=(1,),
        out_shape=jax.ShapeDtypeStruct((WIDTH, WIDTH), jnp.float32),
        in_specs=[pl.BlockSpec((TILE // GROUP, *diag.shape[1:]), lambda _: (0, 0, 0, 0))],
        out_specs=pl.BlockSpec((WIDTH, WIDTH), lambda _: (0, 0)),
        scratch_shapes=[pltpu.VMEM((WIDTH, WIDTH), jnp.float32)],
        cost_estimate=pl.CostEstimate(
            flops=4 * WIDTH**3, bytes_accessed=12 * WIDTH**2, transcendentals=0
        ),
        name="inverse_factor",
    )(diag)


def solve_rows_kernel(rows_ref, inverse_ref, lower_ref):
    raw = jnp.concatenate(
        [
            jnp.concatenate([rows_ref[:, p, g].reshape(-1, TILE) for p in range(PANELS)], axis=1)
            for g in range(rows_ref.shape[2])
        ],
        axis=0,
    )
    lower_ref[...] = product(raw, inverse_ref[...], ((1,), (1,)))


def solve_rows(rows, inverse):
    count = rows.shape[0] * rows.shape[2] * GROUP
    return pl.pallas_call(
        solve_rows_kernel,
        out_shape=jax.ShapeDtypeStruct((count, WIDTH), jnp.float32),
        cost_estimate=pl.CostEstimate(
            flops=12 * count * WIDTH**2, bytes_accessed=8 * count * WIDTH, transcendentals=0
        ),
        name="solve_rows",
    )(rows, inverse)


def trailing_kernel(place_ref, matrix_ref, lower_ref, cols_ref, inverse_ref, out_ref, solved_ref):
    step = pl.program_id(0)
    grid_rows, grid_cols, row_index, col_index = (place_ref[k] for k in range(4))
    rows_here, cols_count = matrix_ref.shape

    @pl.when(step == 0)
    def _():
        cols = jnp.concatenate(
            [cols_ref[:, p].reshape(TILE, cols_count) for p in range(PANELS)], axis=0
        )
        high, low = split(product(inverse_ref[...], cols, ((1,), (0,))))
        solved_ref[0 * WIDTH : 1 * WIDTH, :] = high
        solved_ref[1 * WIDTH : 2 * WIDTH, :] = low
        solved_ref[2 * WIDTH : 3 * WIDTH, :] = high

    high, low = split(lower_ref[...])
    update = jnp.dot(
        jnp.concatenate([high, high, low], axis=1),
        solved_ref[...],
        preferred_element_type=jnp.float32,
    )
    at_row = lax.broadcasted_iota(jnp.int32, (TILE, TILE), 0)
    at_col = lax.broadcasted_iota(jnp.int32, (TILE, TILE), 1)
    for t in range(rows_here // TILE):
        tile_row = (step * (rows_here // TILE) + t) * grid_rows + row_index
        down = slice(t * TILE, (t + 1) * TILE)
        for b in range(cols_count // TILE):
            across = slice(b * TILE, (b + 1) * TILE)
            tile_col = b * grid_cols + col_index
            value = matrix_ref[down, across] - update[down, across]
            for p in range(PANELS):
                panel = lower_ref[down, p * TILE : (p + 1) * TILE]
                value = jnp.where(tile_col == p, panel, value)
            keep = (tile_row - tile_col) * TILE + at_row - at_col >= 0
            keep = keep | ((tile_row == tile_col) & (tile_col >= PANELS))
            out_ref[down, across] = jnp.where(keep, value, 0.0)


def trailing(place, matrix, lower, cols, inverse):
    rows_count, cols_count = matrix.shape
    rows_step = 2 * TILE
    return pl.pallas_call(
        trailing_kernel,
        grid=(rows_count // rows_step,),
        out_shape=jax.ShapeDtypeStruct(matrix.shape, jnp.float32),
        in_specs=[
            pl.BlockSpec(memory_space=pltpu.SMEM),
            pl.BlockSpec((rows_step, cols_count), lambda t: (t, 0)),
            pl.BlockSpec((rows_step, WIDTH), lambda t: (t, 0)),
            pl.BlockSpec(cols.shape, lambda t: (0, 0, 0, 0)),
            pl.BlockSpec(inverse.shape, lambda t: (0, 0)),
        ],
        out_specs=pl.BlockSpec((rows_step, cols_count), lambda t: (t, 0)),
        scratch_shapes=[pltpu.VMEM((3 * WIDTH, cols_count), jnp.bfloat16)],
        name="trailing",
    )(place, matrix, lower, cols, inverse)


def exchange(chunks, axis):
    return lax.all_to_all(chunks, axis, 0, 0, tiled=True)


def to_all(part, axis):
    count = lax.axis_size(axis)
    return exchange(jnp.broadcast_to(part[None], (count, *part.shape)), axis)


def on_device(matrix):
    rows_count, cols_count = matrix.shape
    grid_rows = lax.axis_size("row")
    grid_cols = lax.axis_size("col")
    groups = rows_count // (grid_cols * GROUP)
    with jax.named_scope("scatter_rows"):
        panel = matrix[:, :TILE].reshape(groups, grid_cols, GROUP, TILE).transpose(1, 0, 2, 3)
        row_part = exchange(panel, "col")[:PANELS]
    with jax.named_scope("gather_rows"):
        rows = lax.all_gather(row_part, "col")
    with jax.named_scope("scatter_cols"):
        own_diag = row_part[:, 0].transpose(1, 0, 2).reshape(1, GROUP, PANELS * TILE)
        to_rows = jnp.concatenate(
            [
                matrix[:TILE].reshape(grid_rows, GROUP, cols_count),
                jnp.broadcast_to(own_diag, (grid_rows, *own_diag.shape[1:])),
            ],
            axis=2,
        )
        from_rows = exchange(to_rows, "row")[:PANELS]
        col_part = from_rows[:, :, :cols_count]
        diag_part = from_rows[:, :, cols_count:]
    with jax.named_scope("spread_diagonal"):
        diag = to_all(diag_part, "col")
    with jax.named_scope("gather_cols"):
        diag, col_part = lax.optimization_barrier((diag, col_part))
        cols = to_all(col_part, "row")
    inverse = inverse_factor(diag)
    lower = solve_rows(rows, inverse)
    place = jnp.stack(
        [jnp.int32(grid_rows), jnp.int32(grid_cols), lax.axis_index("row"), lax.axis_index("col")]
    ).astype(jnp.int32)
    return trailing(place, matrix, lower, cols, inverse)


def solution(mesh):
    return jax.shard_map(
        on_device, mesh=mesh, in_specs=(P("row", "col"),), out_specs=P("row", "col"), check_vma=False
    )
```

```python
import jax
import jax.numpy as jnp
from jax import lax
from jax.experimental import pallas as pl
from jax.experimental.pallas import tpu as pltpu
from jax.sharding import PartitionSpec as P

TILE = 128
PANELS = 2
WIDTH = TILE * PANELS
STRIP = 32
GROUP = 8
HIGHEST = lax.Precision.HIGHEST


def product(lhs, rhs, contract):
    return lax.dot_general(
        lhs, rhs, (contract, ((), ())), precision=HIGHEST, preferred_element_type=jnp.float32
    )


def split(value):
    high = value.astype(jnp.bfloat16)
    return high, (value - high.astype(jnp.float32)).astype(jnp.bfloat16)


def eliminate(strip, pivot_lane):
    tiles = [strip[t * GROUP : (t + 1) * GROUP] for t in range(STRIP // GROUP)]
    sub_row = lax.broadcasted_iota(jnp.int32, (GROUP, 1), 0)
    scales = [jnp.ones((GROUP, 1), jnp.float32) for _ in tiles]
    for i in range(STRIP):
        lane = pivot_lane + i
        own, sub = divmod(i, GROUP)
        row = tiles[own][sub : sub + 1, :]
        pivot = tiles[own][sub : sub + 1, lane : lane + 1]
        inverse = 1.0 / pivot
        scales[own] = jnp.where(sub_row == sub, lax.rsqrt(pivot), scales[own])
        for t in range(own, STRIP // GROUP):
            factor = tiles[t][:, lane : lane + 1] * inverse
            if t == own:
                factor = jnp.where(sub_row > sub, factor, 0.0)
            tiles[t] = tiles[t] - factor * row
    return jnp.concatenate([tile * scale for tile, scale in zip(tiles, scales)], axis=0)


def inverse_factor_kernel(diag_ref, inverse_ref, work_ref):
    half = diag_ref.shape[0] // PANELS
    for p in range(PANELS):
        for q in range(PANELS):
            part = diag_ref[q * half : (q + 1) * half, 0, p].reshape(TILE, TILE)
            work_ref[p * TILE : (p + 1) * TILE, q * TILE : (q + 1) * TILE] = part
    at_row = lax.broadcasted_iota(jnp.int32, (WIDTH, WIDTH), 0)
    at_col = lax.broadcasted_iota(jnp.int32, (WIDTH, WIDTH), 1)
    inverse_ref[...] = jnp.where(at_row == at_col, 1.0, 0.0).astype(jnp.float32)
    for start in range(0, WIDTH, STRIP):
        stop = start + STRIP
        first = start // TILE * TILE
        upper = WIDTH - first
        done = first + TILE
        strip = jnp.concatenate(
            [work_ref[start:stop, first:], inverse_ref[start:stop, :done]], axis=1
        )
        strip = eliminate(strip, start - first)
        inverse_ref[start:stop, :done] = strip[:, upper:]
        if stop < WIDTH:
            update = product(strip[:, :upper], strip, ((0,), (0,)))[stop - first :]
            work_ref[stop:, first:] = work_ref[stop:, first:] - update[:, :upper]
            inverse_ref[stop:, :done] = inverse_ref[stop:, :done] - update[:, upper:]


def inverse_factor(diag):
    return pl.pallas_call(
        inverse_factor_kernel,
        grid=(1,),
        out_shape=jax.ShapeDtypeStruct((WIDTH, WIDTH), jnp.float32),
        in_specs=[pl.BlockSpec((diag.shape[0], 1, *diag.shape[2:]), lambda _: (0, 0, 0, 0, 0))],
        out_specs=pl.BlockSpec((WIDTH, WIDTH), lambda _: (0, 0)),
        scratch_shapes=[pltpu.VMEM((WIDTH, WIDTH), jnp.float32)],
        cost_estimate=pl.CostEstimate(
            flops=4 * WIDTH**3, bytes_accessed=12 * WIDTH**2, transcendentals=0
        ),
        name="inverse_factor",
    )(diag)


def solve_rows_kernel(first_ref, rest_ref, inverse_ref, lower_ref):
    half = first_ref.shape[0] // PANELS
    raw = []
    for t in range(lower_ref.shape[0] // TILE):
        group, tile = divmod(t, PANELS)
        parts = []
        for p in range(PANELS):
            side = (tile + p) % PANELS
            held = slice(side * half, (side + 1) * half)
            part = first_ref[held, 1, p] if group == 0 else rest_ref[held, p, group - 1]
            parts.append(part.reshape(TILE, TILE))
        raw.append(jnp.concatenate(parts, axis=1))
    lower_ref[...] = product(jnp.concatenate(raw, axis=0), inverse_ref[...], ((1,), (1,)))


def solve_rows(first, rest, inverse):
    count = rest.shape[0] * (rest.shape[2] + 1) * GROUP
    return pl.pallas_call(
        solve_rows_kernel,
        out_shape=jax.ShapeDtypeStruct((count, WIDTH), jnp.float32),
        cost_estimate=pl.CostEstimate(
            flops=12 * count * WIDTH**2, bytes_accessed=8 * count * WIDTH, transcendentals=0
        ),
        name="solve_rows",
    )(first, rest, inverse)


def trailing_kernel(place_ref, matrix_ref, lower_ref, cols_ref, inverse_ref, out_ref, solved_ref):
    step = pl.program_id(0)
    grid_rows, grid_cols, row_index, col_index = (place_ref[k] for k in range(4))
    rows_here, cols_count = matrix_ref.shape

    @pl.when(step == 0)
    def _():
        cols = jnp.concatenate(
            [cols_ref[:, p].reshape(TILE, cols_count) for p in range(PANELS)], axis=0
        )
        high, low = split(product(inverse_ref[...], cols, ((1,), (0,))))
        solved_ref[0 * WIDTH : 1 * WIDTH, :] = high
        solved_ref[1 * WIDTH : 2 * WIDTH, :] = low
        solved_ref[2 * WIDTH : 3 * WIDTH, :] = high

    high, low = split(lower_ref[...])
    update = jnp.dot(
        jnp.concatenate([high, high, low], axis=1),
        solved_ref[...],
        preferred_element_type=jnp.float32,
    )
    at_row = lax.broadcasted_iota(jnp.int32, (TILE, TILE), 0)
    at_col = lax.broadcasted_iota(jnp.int32, (TILE, TILE), 1)
    for t in range(rows_here // TILE):
        tile_row = (step * (rows_here // TILE) + t) * grid_rows + row_index
        down = slice(t * TILE, (t + 1) * TILE)
        for b in range(cols_count // TILE):
            across = slice(b * TILE, (b + 1) * TILE)
            tile_col = b * grid_cols + col_index
            value = matrix_ref[down, across] - update[down, across]
            for p in range(PANELS):
                panel = lower_ref[down, p * TILE : (p + 1) * TILE]
                value = jnp.where(tile_col == p, panel, value)
            keep = (tile_row - tile_col) * TILE + at_row - at_col >= 0
            keep = keep | ((tile_row == tile_col) & (tile_col >= PANELS))
            out_ref[down, across] = jnp.where(keep, value, 0.0)


def trailing(place, matrix, lower, cols, inverse):
    rows_count, cols_count = matrix.shape
    rows_step = 2 * TILE
    return pl.pallas_call(
        trailing_kernel,
        grid=(rows_count // rows_step,),
        out_shape=jax.ShapeDtypeStruct(matrix.shape, jnp.float32),
        in_specs=[
            pl.BlockSpec(memory_space=pltpu.SMEM),
            pl.BlockSpec((rows_step, cols_count), lambda t: (t, 0)),
            pl.BlockSpec((rows_step, WIDTH), lambda t: (t, 0)),
            pl.BlockSpec(cols.shape, lambda t: (0, 0, 0, 0)),
            pl.BlockSpec(inverse.shape, lambda t: (0, 0)),
        ],
        out_specs=pl.BlockSpec((rows_step, cols_count), lambda t: (t, 0)),
        scratch_shapes=[pltpu.VMEM((3 * WIDTH, cols_count), jnp.bfloat16)],
        name="trailing",
    )(place, matrix, lower, cols, inverse)


def exchange(chunks, axis):
    return lax.all_to_all(chunks, axis, 0, 0, tiled=True)


def to_all(part, axis):
    count = lax.axis_size(axis)
    return exchange(jnp.broadcast_to(part[None], (count, *part.shape)), axis)


def on_device(matrix):
    rows_count, cols_count = matrix.shape
    grid_rows = lax.axis_size("row")
    grid_cols = lax.axis_size("col")
    col_index = lax.axis_index("col")
    half = grid_cols // PANELS
    groups = rows_count // (grid_cols * GROUP)
    with jax.named_scope("scatter_rows"):
        panel = matrix[:, :TILE].reshape(groups, PANELS, half, GROUP, TILE)
        panel = jnp.where(col_index == 1, panel[:, ::-1], panel)
        panel = panel.transpose(1, 2, 0, 3, 4).reshape(grid_cols, groups, GROUP, TILE)
        row_part = exchange(panel, "col")[:PANELS]
    with jax.named_scope("scatter_cols"):
        own_diag = jnp.where(col_index < half, row_part[0, 0], row_part[1, 0])
        to_rows = jnp.concatenate(
            [
                matrix[:TILE].reshape(grid_rows, GROUP, cols_count),
                jnp.broadcast_to(own_diag[None], (grid_rows, GROUP, TILE)),
            ],
            axis=2,
        )
        from_rows = exchange(to_rows, "row")[:PANELS]
        col_part = from_rows[:, :, :cols_count]
        diag_part = from_rows[:, :, cols_count:]
    with jax.named_scope("gather_rows"):
        rest = lax.all_gather(row_part[:, 1:], "col")
    with jax.named_scope("spread_diagonal"):
        diag_part, rest = lax.optimization_barrier((diag_part, rest))
        first = to_all(jnp.stack([diag_part, row_part[:, 0]]), "col")
    with jax.named_scope("gather_cols"):
        first, col_part = lax.optimization_barrier((first, col_part))
        cols = to_all(col_part, "row")
    inverse = inverse_factor(first)
    lower = solve_rows(first, rest, inverse)
    place = jnp.stack(
        [jnp.int32(grid_rows), jnp.int32(grid_cols), lax.axis_index("row"), col_index]
    ).astype(jnp.int32)
    return trailing(place, matrix, lower, cols, inverse)


def solution(mesh):
    return jax.shard_map(
        on_device, mesh=mesh, in_specs=(P("row", "col"),), out_specs=P("row", "col"), check_vma=False
    )
```

```python
import jax
import jax.numpy as jnp
from jax import lax
from jax.experimental import pallas as pl
from jax.experimental.pallas import tpu as pltpu
from jax.sharding import PartitionSpec as P

TILE = 128
PANELS = 2
WIDTH = TILE * PANELS
STRIP = 64
GROUP = 8
HIGHEST = lax.Precision.HIGHEST


def product(lhs, rhs, contract):
    return lax.dot_general(
        lhs, rhs, (contract, ((), ())), precision=HIGHEST, preferred_element_type=jnp.float32
    )


def split(value):
    high = value.astype(jnp.bfloat16)
    return high, (value - high.astype(jnp.float32)).astype(jnp.bfloat16)


def eliminate(strip, pivot_lane):
    count, width = strip.shape
    shape = (GROUP, TILE)
    tiles = [
        [strip[t * GROUP : (t + 1) * GROUP, v * TILE : (v + 1) * TILE] for v in range(width // TILE)]
        for t in range(count // GROUP)
    ]
    sub_row = lax.broadcasted_iota(jnp.int32, shape, 0)

    def over_lanes(tile, lane):
        return jnp.broadcast_to(tile[:, lane : lane + 1], shape)

    def over_rows(tile, row):
        return jnp.broadcast_to(tile[row : row + 1], shape)

    scaled = []
    for own in range(len(tiles)):
        block, lane = divmod(pivot_lane + GROUP * own, TILE)
        columns = [
            [over_lanes(parts[block], lane + k) for k in range(GROUP)] for parts in tiles[own:]
        ]
        pivots = jnp.ones(shape, jnp.float32)
        for k in range(GROUP):
            pivot_row = {j: over_rows(columns[0][j], k) for j in range(k, GROUP)}
            inverse = 1.0 / pivot_row[k]
            pivots = jnp.where(sub_row == k, pivot_row[k], pivots)
            rows = [over_rows(part, k) for part in tiles[own]]
            for t, column in enumerate(columns, own):
                factor = column[k] * inverse
                for j in range(k + 1, GROUP):
                    column[j] = column[j] - factor * pivot_row[j]
                if t == own:
                    factor = jnp.where(sub_row > k, factor, 0.0)
                tiles[t] = [part - factor * row for part, row in zip(tiles[t], rows)]
        scale = lax.rsqrt(pivots)
        scaled.append(jnp.concatenate([part * scale for part in tiles[own]], axis=1))
    return jnp.concatenate(scaled, axis=0)


def inverse_factor_kernel(diag_ref, inverse_ref, work_ref):
    half = diag_ref.shape[0] // PANELS
    for p in range(PANELS):
        for q in range(PANELS):
            part = diag_ref[q * half : (q + 1) * half, p, 0].reshape(TILE, TILE)
            work_ref[p * TILE : (p + 1) * TILE, q * TILE : (q + 1) * TILE] = part
    at_row = lax.broadcasted_iota(jnp.int32, (WIDTH, WIDTH), 0)
    at_col = lax.broadcasted_iota(jnp.int32, (WIDTH, WIDTH), 1)
    inverse_ref[...] = jnp.where(at_row == at_col, 1.0, 0.0).astype(jnp.float32)
    for start in range(0, WIDTH, STRIP):
        stop = start + STRIP
        first = start // TILE * TILE
        upper = WIDTH - first
        done = first + TILE
        strip = jnp.concatenate(
            [work_ref[start:stop, first:], inverse_ref[start:stop, :done]], axis=1
        )
        strip = eliminate(strip, start - first)
        inverse_ref[start:stop, :done] = strip[:, upper:]
        if stop < WIDTH:
            update = product(strip[:, :upper], strip, ((0,), (0,)))[stop - first :]
            work_ref[stop:, first:] = work_ref[stop:, first:] - update[:, :upper]
            inverse_ref[stop:, :done] = inverse_ref[stop:, :done] - update[:, upper:]


def inverse_factor(held):
    return pl.pallas_call(
        inverse_factor_kernel,
        grid=(1,),
        out_shape=jax.ShapeDtypeStruct((WIDTH, WIDTH), jnp.float32),
        in_specs=[pl.BlockSpec((*held.shape[:2], 1, GROUP, TILE), lambda _: (0, 0, 0, 0, 0))],
        out_specs=pl.BlockSpec((WIDTH, WIDTH), lambda _: (0, 0)),
        scratch_shapes=[pltpu.VMEM((WIDTH, WIDTH), jnp.float32)],
        cost_estimate=pl.CostEstimate(
            flops=4 * WIDTH**3, bytes_accessed=12 * WIDTH**2, transcendentals=0
        ),
        name="inverse_factor",
    )(held)


def solve_rows_kernel(held_ref, inverse_ref, lower_ref):
    half = held_ref.shape[0] // PANELS
    raw = []
    for t in range(lower_ref.shape[0] // TILE):
        group, tile = divmod(t, PANELS)
        parts = []
        for p in range(PANELS):
            side = (tile + p) % PANELS
            part = held_ref[side * half : (side + 1) * half, p, group + 1]
            parts.append(part.reshape(TILE, TILE))
        raw.append(jnp.concatenate(parts, axis=1))
    lower_ref[...] = product(jnp.concatenate(raw, axis=0), inverse_ref[...], ((1,), (1,)))


def solve_rows(held, inverse):
    count = held.shape[0] * (held.shape[2] - 1) * GROUP
    return pl.pallas_call(
        solve_rows_kernel,
        out_shape=jax.ShapeDtypeStruct((count, WIDTH), jnp.float32),
        cost_estimate=pl.CostEstimate(
            flops=12 * count * WIDTH**2, bytes_accessed=8 * count * WIDTH, transcendentals=0
        ),
        name="solve_rows",
    )(held, inverse)


def trailing_kernel(place_ref, matrix_ref, lower_ref, cols_ref, inverse_ref, out_ref, solved_ref):
    step = pl.program_id(0)
    grid_rows, grid_cols, row_index, col_index = (place_ref[k] for k in range(4))
    rows_here, cols_count = matrix_ref.shape

    @pl.when(step == 0)
    def _():
        cols = jnp.concatenate(
            [cols_ref[:, p].reshape(TILE, cols_count) for p in range(PANELS)], axis=0
        )
        high, low = split(product(inverse_ref[...], cols, ((1,), (0,))))
        solved_ref[0 * WIDTH : 1 * WIDTH, :] = high
        solved_ref[1 * WIDTH : 2 * WIDTH, :] = low
        solved_ref[2 * WIDTH : 3 * WIDTH, :] = high

    high, low = split(lower_ref[...])
    update = jnp.dot(
        jnp.concatenate([high, high, low], axis=1),
        solved_ref[...],
        preferred_element_type=jnp.float32,
    )
    at_row = lax.broadcasted_iota(jnp.int32, (TILE, TILE), 0)
    at_col = lax.broadcasted_iota(jnp.int32, (TILE, TILE), 1)
    for t in range(rows_here // TILE):
        tile_row = (step * (rows_here // TILE) + t) * grid_rows + row_index
        down = slice(t * TILE, (t + 1) * TILE)
        for b in range(cols_count // TILE):
            across = slice(b * TILE, (b + 1) * TILE)
            tile_col = b * grid_cols + col_index
            value = matrix_ref[down, across] - update[down, across]
            for p in range(PANELS):
                panel = lower_ref[down, p * TILE : (p + 1) * TILE]
                value = jnp.where(tile_col == p, panel, value)
            keep = (tile_row - tile_col) * TILE + at_row - at_col >= 0
            keep = keep | ((tile_row == tile_col) & (tile_col >= PANELS))
            out_ref[down, across] = jnp.where(keep, value, 0.0)


def trailing(place, matrix, lower, cols, inverse):
    rows_count, cols_count = matrix.shape
    rows_step = 2 * TILE
    return pl.pallas_call(
        trailing_kernel,
        grid=(rows_count // rows_step,),
        out_shape=jax.ShapeDtypeStruct(matrix.shape, jnp.float32),
        in_specs=[
            pl.BlockSpec(memory_space=pltpu.SMEM),
            pl.BlockSpec((rows_step, cols_count), lambda t: (t, 0)),
            pl.BlockSpec((rows_step, WIDTH), lambda t: (t, 0)),
            pl.BlockSpec(cols.shape, lambda t: (0, 0, 0, 0)),
            pl.BlockSpec(inverse.shape, lambda t: (0, 0)),
        ],
        out_specs=pl.BlockSpec((rows_step, cols_count), lambda t: (t, 0)),
        scratch_shapes=[pltpu.VMEM((3 * WIDTH, cols_count), jnp.bfloat16)],
        name="trailing",
    )(place, matrix, lower, cols, inverse)


def exchange(chunks, axis):
    return lax.all_to_all(chunks, axis, 0, 0, tiled=True)


def to_all(part, axis):
    count = lax.axis_size(axis)
    return exchange(jnp.broadcast_to(part[None], (count, *part.shape)), axis)


def on_device(matrix):
    rows_count, cols_count = matrix.shape
    grid_rows = lax.axis_size("row")
    grid_cols = lax.axis_size("col")
    col_index = lax.axis_index("col")
    half = grid_cols // PANELS
    groups = rows_count // (grid_cols * GROUP)
    with jax.named_scope("scatter_rows"):
        panel = matrix[:, :TILE].reshape(groups, PANELS, half, GROUP, TILE)
        panel = jnp.where(col_index == 1, panel[:, ::-1], panel)
        panel = panel.transpose(1, 2, 0, 3, 4).reshape(grid_cols, groups, GROUP, TILE)
        row_part = exchange(panel, "col")[:PANELS]
    with jax.named_scope("scatter_cols"):
        own_diag = jnp.where(col_index < half, row_part[0, 0], row_part[1, 0])
        to_rows = jnp.concatenate(
            [
                matrix[:TILE].reshape(grid_rows, GROUP, cols_count),
                jnp.broadcast_to(own_diag[None], (grid_rows, GROUP, TILE)),
            ],
            axis=2,
        )
        from_rows = exchange(to_rows, "row")[:PANELS]
        col_part = from_rows[:, :, :cols_count]
        diag_part = from_rows[:, :, cols_count:]
    with jax.named_scope("gather_rows"):
        held = to_all(jnp.concatenate([diag_part[:, None], row_part], axis=1), "col")
    with jax.named_scope("gather_cols"):
        cols = lax.all_gather(col_part, "row")
    held, cols = lax.optimization_barrier((held, cols))
    inverse = inverse_factor(held)
    lower = solve_rows(held, inverse)
    place = jnp.stack(
        [jnp.int32(grid_rows), jnp.int32(grid_cols), lax.axis_index("row"), col_index]
    ).astype(jnp.int32)
    return trailing(place, matrix, lower, cols, inverse)


def solution(mesh):
    return jax.shard_map(
        on_device, mesh=mesh, in_specs=(P("row", "col"),), out_specs=P("row", "col"), check_vma=False
    )
```

```python
import jax
import jax.numpy as jnp
from jax import lax
from jax.experimental import pallas as pl
from jax.experimental.pallas import tpu as pltpu
from jax.sharding import PartitionSpec as P

TILE = 128
PANELS = 2
WIDTH = TILE * PANELS
STRIP = 64
GROUP = 8
HIGHEST = lax.Precision.HIGHEST


def product(lhs, rhs, contract):
    return lax.dot_general(
        lhs, rhs, (contract, ((), ())), precision=HIGHEST, preferred_element_type=jnp.float32
    )


def split(value):
    high = value.astype(jnp.bfloat16)
    return high, (value - high.astype(jnp.float32)).astype(jnp.bfloat16)


def eliminate(strip, pivot_lane):
    count, width = strip.shape
    shape = (GROUP, TILE)
    tiles = [
        [strip[t * GROUP : (t + 1) * GROUP, v * TILE : (v + 1) * TILE] for v in range(width // TILE)]
        for t in range(count // GROUP)
    ]
    sub_row = lax.broadcasted_iota(jnp.int32, shape, 0)

    def over_lanes(tile, lane):
        return jnp.broadcast_to(tile[:, lane : lane + 1], shape)

    def over_rows(tile, row):
        return jnp.broadcast_to(tile[row : row + 1], shape)

    scaled = []
    for own in range(len(tiles)):
        block, lane = divmod(pivot_lane + GROUP * own, TILE)
        columns = [
            [over_lanes(parts[block], lane + k) for k in range(GROUP)] for parts in tiles[own:]
        ]
        pivots = jnp.ones(shape, jnp.float32)
        for k in range(GROUP):
            pivot_row = {j: over_rows(columns[0][j], k) for j in range(k, GROUP)}
            inverse = 1.0 / pivot_row[k]
            pivots = jnp.where(sub_row == k, pivot_row[k], pivots)
            rows = [over_rows(part, k) for part in tiles[own]]
            for t, column in enumerate(columns, own):
                factor = column[k] * inverse
                for j in range(k + 1, GROUP):
                    column[j] = column[j] - factor * pivot_row[j]
                if t == own:
                    factor = jnp.where(sub_row > k, factor, 0.0)
                tiles[t] = [part - factor * row for part, row in zip(tiles[t], rows)]
        scale = lax.rsqrt(pivots)
        scaled.append(jnp.concatenate([part * scale for part in tiles[own]], axis=1))
    return jnp.concatenate(scaled, axis=0)


def inverse_factor_kernel(diag_ref, inverse_ref, work_ref):
    for p in range(PANELS):
        work_ref[p * TILE : (p + 1) * TILE, :] = diag_ref[:, p].reshape(TILE, WIDTH)
    at_row = lax.broadcasted_iota(jnp.int32, (WIDTH, WIDTH), 0)
    at_col = lax.broadcasted_iota(jnp.int32, (WIDTH, WIDTH), 1)
    inverse_ref[...] = jnp.where(at_row == at_col, 1.0, 0.0).astype(jnp.float32)
    for start in range(0, WIDTH, STRIP):
        stop = start + STRIP
        first = start // TILE * TILE
        upper = WIDTH - first
        done = first + TILE
        strip = jnp.concatenate(
            [work_ref[start:stop, first:], inverse_ref[start:stop, :done]], axis=1
        )
        strip = eliminate(strip, start - first)
        inverse_ref[start:stop, :done] = strip[:, upper:]
        if stop < WIDTH:
            update = product(strip[:, :upper], strip, ((0,), (0,)))[stop - first :]
            work_ref[stop:, first:] = work_ref[stop:, first:] - update[:, :upper]
            inverse_ref[stop:, :done] = inverse_ref[stop:, :done] - update[:, upper:]


def inverse_factor(spread):
    last = spread.shape[-1] // WIDTH - 1
    return pl.pallas_call(
        inverse_factor_kernel,
        grid=(1,),
        out_shape=jax.ShapeDtypeStruct((WIDTH, WIDTH), jnp.float32),
        in_specs=[pl.BlockSpec((*spread.shape[:-1], WIDTH), lambda _: (0, 0, 0, last))],
        out_specs=pl.BlockSpec((WIDTH, WIDTH), lambda _: (0, 0)),
        scratch_shapes=[pltpu.VMEM((WIDTH, WIDTH), jnp.float32)],
        cost_estimate=pl.CostEstimate(
            flops=4 * WIDTH**3, bytes_accessed=12 * WIDTH**2, transcendentals=0
        ),
        name="inverse_factor",
    )(spread)


def solve_rows_kernel(held_ref, inverse_ref, lower_ref):
    half = held_ref.shape[0] // PANELS
    raw = []
    for t in range(lower_ref.shape[0] // TILE):
        group, side = divmod(t, PANELS)
        held = slice(side * half, (side + 1) * half)
        parts = [held_ref[held, p, group].reshape(TILE, TILE) for p in range(PANELS)]
        raw.append(jnp.concatenate(parts, axis=1))
    lower_ref[...] = product(jnp.concatenate(raw, axis=0), inverse_ref[...], ((1,), (1,)))


def solve_rows(held, inverse):
    count = held.shape[0] * held.shape[2] * GROUP
    return pl.pallas_call(
        solve_rows_kernel,
        out_shape=jax.ShapeDtypeStruct((count, WIDTH), jnp.float32),
        cost_estimate=pl.CostEstimate(
            flops=12 * count * WIDTH**2, bytes_accessed=8 * count * WIDTH, transcendentals=0
        ),
        name="solve_rows",
    )(held, inverse)


def trailing_kernel(place_ref, matrix_ref, lower_ref, cols_ref, inverse_ref, out_ref, solved_ref):
    step = pl.program_id(0)
    grid_rows, grid_cols, row_index, col_index = (place_ref[k] for k in range(4))
    rows_here, cols_count = matrix_ref.shape

    @pl.when(step == 0)
    def _():
        cols = jnp.concatenate(
            [cols_ref[:, p].reshape(TILE, cols_count) for p in range(PANELS)], axis=0
        )
        high, low = split(product(inverse_ref[...], cols, ((1,), (0,))))
        solved_ref[0 * WIDTH : 1 * WIDTH, :] = high
        solved_ref[1 * WIDTH : 2 * WIDTH, :] = low
        solved_ref[2 * WIDTH : 3 * WIDTH, :] = high

    high, low = split(lower_ref[...])
    update = jnp.dot(
        jnp.concatenate([high, high, low], axis=1),
        solved_ref[...],
        preferred_element_type=jnp.float32,
    )
    at_row = lax.broadcasted_iota(jnp.int32, (TILE, TILE), 0)
    at_col = lax.broadcasted_iota(jnp.int32, (TILE, TILE), 1)
    for t in range(rows_here // TILE):
        tile_row = (step * (rows_here // TILE) + t) * grid_rows + row_index
        down = slice(t * TILE, (t + 1) * TILE)
        for b in range(cols_count // TILE):
            across = slice(b * TILE, (b + 1) * TILE)
            tile_col = b * grid_cols + col_index
            value = matrix_ref[down, across] - update[down, across]
            for p in range(PANELS):
                panel = lower_ref[down, p * TILE : (p + 1) * TILE]
                value = jnp.where(tile_col == p, panel, value)
            keep = (tile_row - tile_col) * TILE + at_row - at_col >= 0
            keep = keep | ((tile_row == tile_col) & (tile_col >= PANELS))
            out_ref[down, across] = jnp.where(keep, value, 0.0)


def trailing(place, matrix, lower, cols, inverse):
    rows_count, cols_count = matrix.shape
    rows_step = 2 * TILE
    return pl.pallas_call(
        trailing_kernel,
        grid=(rows_count // rows_step,),
        out_shape=jax.ShapeDtypeStruct(matrix.shape, jnp.float32),
        in_specs=[
            pl.BlockSpec(memory_space=pltpu.SMEM),
            pl.BlockSpec((rows_step, cols_count), lambda t: (t, 0)),
            pl.BlockSpec((rows_step, WIDTH), lambda t: (t, 0)),
            pl.BlockSpec((*cols.shape[:-1], cols_count), lambda t: (0, 0, 0, 0)),
            pl.BlockSpec(inverse.shape, lambda t: (0, 0)),
        ],
        out_specs=pl.BlockSpec((rows_step, cols_count), lambda t: (t, 0)),
        scratch_shapes=[pltpu.VMEM((3 * WIDTH, cols_count), jnp.bfloat16)],
        name="trailing",
    )(place, matrix, lower, cols, inverse)


def exchange(chunks, axis):
    return lax.all_to_all(chunks, axis, 0, 0, tiled=True)


def to_all(part, axis):
    count = lax.axis_size(axis)
    return exchange(jnp.broadcast_to(part[None], (count, *part.shape)), axis)


def on_device(matrix):
    rows_count, cols_count = matrix.shape
    grid_rows = lax.axis_size("row")
    grid_cols = lax.axis_size("col")
    groups = rows_count // (grid_cols * GROUP)
    with jax.named_scope("scatter_cols"):
        to_rows = matrix[:TILE].reshape(grid_rows, GROUP, cols_count)
        col_part = exchange(to_rows, "row")[:PANELS]
    with jax.named_scope("scatter_rows"):
        panel = matrix[:, :TILE].reshape(groups, grid_cols, GROUP, TILE).transpose(1, 0, 2, 3)
        own_diag = jnp.broadcast_to(col_part[None, :, :, :TILE], (grid_cols, PANELS, GROUP, TILE))
        from_cols = exchange(jnp.concatenate([panel, own_diag], axis=1), "col")[:PANELS]
        row_part = from_cols[:, :groups]
        diag_part = from_cols[:, groups:].transpose(1, 2, 0, 3).reshape(PANELS, GROUP, WIDTH)
    with jax.named_scope("gather_rows"):
        held = to_all(row_part, "col")
    with jax.named_scope("gather_cols"):
        spread = lax.all_gather(jnp.concatenate([col_part, diag_part], axis=2), "row")
    held, spread = lax.optimization_barrier((held, spread))
    inverse = inverse_factor(spread)
    lower = solve_rows(held, inverse)
    place = jnp.stack(
        [jnp.int32(grid_rows), jnp.int32(grid_cols), lax.axis_index("row"), lax.axis_index("col")]
    ).astype(jnp.int32)
    return trailing(place, matrix, lower, spread, inverse)


def solution(mesh):
    return jax.shard_map(
        on_device, mesh=mesh, in_specs=(P("row", "col"),), out_specs=P("row", "col"), check_vma=False
    )
```

```python
import jax
import jax.numpy as jnp
from jax import lax
from jax.experimental import pallas as pl
from jax.experimental.pallas import tpu as pltpu
from jax.sharding import PartitionSpec as P

TILE = 128
PANELS = 2
WIDTH = TILE * PANELS
STRIP = 64
GROUP = 8
HIGHEST = lax.Precision.HIGHEST


def product(lhs, rhs, contract):
    return lax.dot_general(
        lhs, rhs, (contract, ((), ())), precision=HIGHEST, preferred_element_type=jnp.float32
    )


def split(value):
    high = value.astype(jnp.bfloat16)
    return high, (value - high.astype(jnp.float32)).astype(jnp.bfloat16)


def eliminate(strip, pivot_lane):
    count, width = strip.shape
    shape = (GROUP, TILE)
    tiles = [
        [strip[t * GROUP : (t + 1) * GROUP, v * TILE : (v + 1) * TILE] for v in range(width // TILE)]
        for t in range(count // GROUP)
    ]
    sub_row = lax.broadcasted_iota(jnp.int32, shape, 0)

    def over_lanes(tile, lane):
        return jnp.broadcast_to(tile[:, lane : lane + 1], shape)

    def over_rows(tile, row):
        return jnp.broadcast_to(tile[row : row + 1], shape)

    scaled = []
    for own in range(len(tiles)):
        block, lane = divmod(pivot_lane + GROUP * own, TILE)
        columns = [
            [over_lanes(parts[block], lane + k) for k in range(GROUP)] for parts in tiles[own:]
        ]
        pivots = jnp.ones(shape, jnp.float32)
        for k in range(GROUP):
            pivot_row = {j: over_rows(columns[0][j], k) for j in range(k, GROUP)}
            inverse = 1.0 / pivot_row[k]
            pivots = jnp.where(sub_row == k, pivot_row[k], pivots)
            rows = [over_rows(part, k) for part in tiles[own]]
            for t, column in enumerate(columns, own):
                factor = column[k] * inverse
                for j in range(k + 1, GROUP):
                    column[j] = column[j] - factor * pivot_row[j]
                if t == own:
                    factor = jnp.where(sub_row > k, factor, 0.0)
                tiles[t] = [part - factor * row for part, row in zip(tiles[t], rows)]
        scale = lax.rsqrt(pivots)
        scaled.append(jnp.concatenate([part * scale for part in tiles[own]], axis=1))
    return jnp.concatenate(scaled, axis=0)


def inverse_factor_kernel(diag_ref, inverse_ref, work_ref):
    half = diag_ref.shape[0] // PANELS
    for p in range(PANELS):
        for q in range(PANELS):
            part = diag_ref[q * half : (q + 1) * half, p].reshape(TILE, TILE)
            work_ref[p * TILE : (p + 1) * TILE, q * TILE : (q + 1) * TILE] = part
    at_row = lax.broadcasted_iota(jnp.int32, (WIDTH, WIDTH), 0)
    at_col = lax.broadcasted_iota(jnp.int32, (WIDTH, WIDTH), 1)
    inverse_ref[...] = jnp.where(at_row == at_col, 1.0, 0.0).astype(jnp.float32)
    for start in range(0, WIDTH, STRIP):
        stop = start + STRIP
        first = start // TILE * TILE
        upper = WIDTH - first
        done = first + TILE
        strip = jnp.concatenate(
            [work_ref[start:stop, first:], inverse_ref[start:stop, :done]], axis=1
        )
        strip = eliminate(strip, start - first)
        inverse_ref[start:stop, :done] = strip[:, upper:]
        if stop < WIDTH:
            update = product(strip[:, :upper], strip, ((0,), (0,)))[stop - first :]
            work_ref[stop:, first:] = work_ref[stop:, first:] - update[:, :upper]
            inverse_ref[stop:, :done] = inverse_ref[stop:, :done] - update[:, upper:]


def inverse_factor(diag):
    return pl.pallas_call(
        inverse_factor_kernel,
        out_shape=jax.ShapeDtypeStruct((WIDTH, WIDTH), jnp.float32),
        scratch_shapes=[pltpu.VMEM((WIDTH, WIDTH), jnp.float32)],
        cost_estimate=pl.CostEstimate(
            flops=4 * WIDTH**3, bytes_accessed=12 * WIDTH**2, transcendentals=0
        ),
        name="inverse_factor",
    )(diag)


def solve_rows_kernel(held_ref, inverse_ref, lower_ref):
    half = held_ref.shape[0] // PANELS
    raw = []
    for t in range(lower_ref.shape[0] // TILE):
        group, tile = divmod(t, PANELS)
        parts = []
        for p in range(PANELS):
            side = (tile + p) % PANELS
            part = held_ref[side * half : (side + 1) * half, p, group]
            parts.append(part.reshape(TILE, TILE))
        raw.append(jnp.concatenate(parts, axis=1))
    lower_ref[...] = product(jnp.concatenate(raw, axis=0), inverse_ref[...], ((1,), (1,)))


def solve_rows(held, inverse):
    count = held.shape[0] * held.shape[2] * GROUP
    return pl.pallas_call(
        solve_rows_kernel,
        out_shape=jax.ShapeDtypeStruct((count, WIDTH), jnp.float32),
        cost_estimate=pl.CostEstimate(
            flops=12 * count * WIDTH**2, bytes_accessed=8 * count * WIDTH, transcendentals=0
        ),
        name="solve_rows",
    )(held, inverse)


def trailing_kernel(place_ref, matrix_ref, lower_ref, cols_ref, inverse_ref, out_ref, solved_ref):
    step = pl.program_id(0)
    grid_rows, grid_cols, row_index, col_index = (place_ref[k] for k in range(4))
    rows_here, cols_count = matrix_ref.shape

    @pl.when(step == 0)
    def _():
        half = cols_ref.shape[0] // PANELS
        sides = [
            jnp.concatenate(
                [
                    cols_ref[q * half : (q + 1) * half, b].reshape(TILE, TILE)
                    for b in range(cols_ref.shape[1])
                ],
                axis=0,
            )
            for q in range(PANELS)
        ]
        low_half = col_index < half
        raw = jnp.concatenate(
            [
                jnp.where(low_half, sides[0], sides[1]),
                jnp.where(low_half, sides[1], sides[0]),
            ],
            axis=1,
        )
        high, low = split(product(raw, inverse_ref[...], ((1,), (1,))))
        solved_ref[:, 0 * WIDTH : 1 * WIDTH] = high
        solved_ref[:, 1 * WIDTH : 2 * WIDTH] = low
        solved_ref[:, 2 * WIDTH : 3 * WIDTH] = high

    high, low = split(lower_ref[...])
    update = lax.dot_general(
        jnp.concatenate([high, high, low], axis=1),
        solved_ref[...],
        (((1,), (1,)), ((), ())),
        preferred_element_type=jnp.float32,
    )
    at_row = lax.broadcasted_iota(jnp.int32, (TILE, TILE), 0)
    at_col = lax.broadcasted_iota(jnp.int32, (TILE, TILE), 1)
    for t in range(rows_here // TILE):
        tile_row = (step * (rows_here // TILE) + t) * grid_rows + row_index
        down = slice(t * TILE, (t + 1) * TILE)
        for b in range(cols_count // TILE):
            across = slice(b * TILE, (b + 1) * TILE)
            tile_col = b * grid_cols + col_index
            value = matrix_ref[down, across] - update[down, across]
            for p in range(PANELS):
                panel = lower_ref[down, p * TILE : (p + 1) * TILE]
                value = jnp.where(tile_col == p, panel, value)
            keep = (tile_row - tile_col) * TILE + at_row - at_col >= 0
            keep = keep | ((tile_row == tile_col) & (tile_col >= PANELS))
            out_ref[down, across] = jnp.where(keep, value, 0.0)


def trailing(place, matrix, lower, cols, inverse):
    rows_count, cols_count = matrix.shape
    rows_step = 2 * TILE
    return pl.pallas_call(
        trailing_kernel,
        grid=(rows_count // rows_step,),
        out_shape=jax.ShapeDtypeStruct(matrix.shape, jnp.float32),
        in_specs=[
            pl.BlockSpec(memory_space=pltpu.SMEM),
            pl.BlockSpec((rows_step, cols_count), lambda t: (t, 0)),
            pl.BlockSpec((rows_step, WIDTH), lambda t: (t, 0)),
            pl.BlockSpec(cols.shape, lambda t: (0, 0, 0, 0)),
            pl.BlockSpec(inverse.shape, lambda t: (0, 0)),
        ],
        out_specs=pl.BlockSpec((rows_step, cols_count), lambda t: (t, 0)),
        scratch_shapes=[pltpu.VMEM((cols_count, 3 * WIDTH), jnp.bfloat16)],
        name="trailing",
    )(place, matrix, lower, cols, inverse)


def exchange(chunks, axis):
    return lax.all_to_all(chunks, axis, 0, 0, tiled=True)


def to_all(part, axis):
    count = lax.axis_size(axis)
    return exchange(jnp.broadcast_to(part[None], (count, *part.shape)), axis)


def on_device(matrix):
    rows_count, cols_count = matrix.shape
    grid_rows = lax.axis_size("row")
    grid_cols = lax.axis_size("col")
    col_index = lax.axis_index("col")
    half = grid_cols // PANELS
    groups = rows_count // (grid_cols * GROUP)
    with jax.named_scope("scatter_rows"):
        panel = matrix[:, :TILE].reshape(groups, PANELS, half, GROUP, TILE)
        panel = jnp.where(col_index == 1, panel[:, ::-1], panel)
        panel = panel.transpose(1, 2, 0, 3, 4).reshape(grid_cols, groups, GROUP, TILE)
        row_part = exchange(panel, "col")[:PANELS]
    with jax.named_scope("gather_rows"):
        held = to_all(row_part, "col")
    with jax.named_scope("gather_planes"):
        planes = lax.all_gather(row_part, "row")
        held, planes = lax.optimization_barrier((held, planes))
    low_half = col_index < half
    with jax.named_scope("spread_diagonal"):
        own = planes[:PANELS, :, 0]
        diag = to_all(jnp.where(low_half, own[:, 0], own[:, 1]), "col")
    with jax.named_scope("exchange_cols"):
        diag, planes = lax.optimization_barrier((diag, planes))
        parts = jnp.where(low_half, planes.swapaxes(0, 1), planes.swapaxes(0, 1)[::-1])
        cols = exchange(parts.reshape(grid_cols, groups, GROUP, TILE), "col")
    inverse = inverse_factor(diag)
    lower = solve_rows(held, inverse)
    place = jnp.stack(
        [jnp.int32(grid_rows), jnp.int32(grid_cols), lax.axis_index("row"), col_index]
    ).astype(jnp.int32)
    return trailing(place, matrix, lower, cols, inverse)


def solution(mesh):
    return jax.shard_map(
        on_device, mesh=mesh, in_specs=(P("row", "col"),), out_specs=P("row", "col"), check_vma=False
    )
```

```python
import functools

import jax
import jax.numpy as jnp
from jax import lax
from jax.experimental import pallas as pl
from jax.experimental.pallas import tpu as pltpu
from jax.sharding import PartitionSpec as P

TILE = 128
PANELS = 2
WIDTH = TILE * PANELS
STRIP = 64
GROUP = 8
HIGHEST = lax.Precision.HIGHEST


def product(lhs, rhs, contract):
    return lax.dot_general(
        lhs, rhs, (contract, ((), ())), precision=HIGHEST, preferred_element_type=jnp.float32
    )


def split(value):
    high = value.astype(jnp.bfloat16)
    return high, (value - high.astype(jnp.float32)).astype(jnp.bfloat16)


def eliminate(strip, pivot_lane):
    count, width = strip.shape
    shape = (GROUP, TILE)
    tiles = [
        [strip[t * GROUP : (t + 1) * GROUP, v * TILE : (v + 1) * TILE] for v in range(width // TILE)]
        for t in range(count // GROUP)
    ]
    sub_row = lax.broadcasted_iota(jnp.int32, shape, 0)

    def over_lanes(tile, lane):
        return jnp.broadcast_to(tile[:, lane : lane + 1], shape)

    def over_rows(tile, row):
        return jnp.broadcast_to(tile[row : row + 1], shape)

    scaled = []
    for own in range(len(tiles)):
        block, lane = divmod(pivot_lane + GROUP * own, TILE)
        columns = [
            [over_lanes(parts[block], lane + k) for k in range(GROUP)] for parts in tiles[own:]
        ]
        pivots = jnp.ones(shape, jnp.float32)
        for k in range(GROUP):
            pivot_row = {j: over_rows(columns[0][j], k) for j in range(k, GROUP)}
            inverse = 1.0 / pivot_row[k]
            pivots = jnp.where(sub_row == k, pivot_row[k], pivots)
            rows = [over_rows(part, k) for part in tiles[own]]
            for t, column in enumerate(columns, own):
                factor = column[k] * inverse
                for j in range(k + 1, GROUP):
                    column[j] = column[j] - factor * pivot_row[j]
                if t == own:
                    factor = jnp.where(sub_row > k, factor, 0.0)
                tiles[t] = [part - factor * row for part, row in zip(tiles[t], rows)]
        scale = lax.rsqrt(pivots)
        scaled.append(jnp.concatenate([part * scale for part in tiles[own]], axis=1))
    return jnp.concatenate(scaled, axis=0)


def panels_kernel(diag_ref, held_ref, inverse_ref, lower_ref, work_ref, raw_ref, sem):
    fetch = pltpu.make_async_copy(held_ref, raw_ref, sem)
    fetch.start()
    for p in range(PANELS):
        for q in range(PANELS):
            part = diag_ref[:, q, p].reshape(TILE, TILE)
            work_ref[p * TILE : (p + 1) * TILE, q * TILE : (q + 1) * TILE] = part
    at_row = lax.broadcasted_iota(jnp.int32, (WIDTH, WIDTH), 0)
    at_col = lax.broadcasted_iota(jnp.int32, (WIDTH, WIDTH), 1)
    inverse_ref[...] = jnp.where(at_row == at_col, 1.0, 0.0).astype(jnp.float32)
    tile_rows = lower_ref.shape[0] // TILE
    for start in range(0, WIDTH, STRIP):
        stop = start + STRIP
        first = start // TILE * TILE
        upper = WIDTH - first
        done = first + TILE
        strip = jnp.concatenate(
            [work_ref[start:stop, first:], inverse_ref[start:stop, :done]], axis=1
        )
        strip = eliminate(strip, start - first)
        inverse_ref[start:stop, :done] = strip[:, upper:]
        if stop < WIDTH:
            update = product(strip[:, :upper], strip, ((0,), (0,)))[stop - first :]
            work_ref[stop:, first:] = work_ref[stop:, first:] - update[:, :upper]
            inverse_ref[stop:, :done] = inverse_ref[stop:, :done] - update[:, upper:]
        if stop % TILE == 0:
            if first == 0:
                fetch.wait()
            raw = jnp.concatenate(
                [
                    jnp.concatenate(
                        [raw_ref[:, p, t].reshape(TILE, TILE) for t in range(tile_rows)], axis=0
                    )
                    for p in range(done // TILE)
                ],
                axis=1,
            )
            lower_ref[:, first:done] = product(raw, inverse_ref[first:done, :done], ((1,), (1,)))


def panels(diag, held):
    count = held.shape[0] * held.shape[2] * GROUP
    return pl.pallas_call(
        panels_kernel,
        out_shape=[
            jax.ShapeDtypeStruct((WIDTH, WIDTH), jnp.float32),
            jax.ShapeDtypeStruct((count, WIDTH), jnp.float32),
        ],
        in_specs=[pl.BlockSpec(memory_space=pltpu.VMEM), pl.BlockSpec(memory_space=pl.ANY)],
        scratch_shapes=[
            pltpu.VMEM((WIDTH, WIDTH), jnp.float32),
            pltpu.VMEM(held.shape, jnp.float32),
            pltpu.SemaphoreType.DMA,
        ],
        cost_estimate=pl.CostEstimate(
            flops=4 * WIDTH**3 + 12 * count * WIDTH**2,
            bytes_accessed=12 * WIDTH**2 + 8 * count * WIDTH,
            transcendentals=0,
        ),
        name="panels",
    )(diag, held)


def trailing_kernel(
    grid_rows, grid_cols, place_ref, matrix_ref, lower_ref, cols_ref, inverse_ref, out_ref, solved_ref
):
    step = pl.program_id(0)
    row_index, col_index = place_ref[0], place_ref[1]
    rows_here, cols_count = matrix_ref.shape
    tile_cols = cols_count // TILE
    tiles_here = rows_here // TILE

    @pl.when(step == 0)
    def _():
        raw = jnp.concatenate(
            [
                jnp.concatenate(
                    [cols_ref[:, p, b].reshape(TILE, TILE) for b in range(tile_cols)], axis=0
                )
                for p in range(PANELS)
            ],
            axis=1,
        )
        high, low = split(product(raw, inverse_ref[...], ((1,), (1,))))
        solved_ref[:, 0 * WIDTH : 1 * WIDTH] = high
        solved_ref[:, 1 * WIDTH : 2 * WIDTH] = low
        solved_ref[:, 2 * WIDTH : 3 * WIDTH] = high

    at_row = lax.broadcasted_iota(jnp.int32, (TILE, TILE), 0)
    at_col = lax.broadcasted_iota(jnp.int32, (TILE, TILE), 1)

    def rows_of(at):
        last_tile_row = ((at + 1) * tiles_here - 1) * grid_rows + grid_rows - 1
        reach = min(tile_cols, last_tile_row // grid_cols + 1)
        high, low = split(lower_ref[...])
        update = lax.dot_general(
            jnp.concatenate([high, high, low], axis=1),
            solved_ref[: reach * TILE, :],
            (((1,), (1,)), ((), ())),
            preferred_element_type=jnp.float32,
        )
        for t in range(tiles_here):
            tile_row = (at * tiles_here + t) * grid_rows + row_index
            down = slice(t * TILE, (t + 1) * TILE)
            for b in range(reach):
                across = slice(b * TILE, (b + 1) * TILE)
                tile_col = b * grid_cols + col_index
                value = matrix_ref[down, across] - update[down, across]
                keep = tile_row >= tile_col
                if b * grid_cols < PANELS:
                    for p in range(PANELS):
                        panel = lower_ref[down, p * TILE : (p + 1) * TILE]
                        value = jnp.where(tile_col == p, panel, value)
                    inner = (tile_row - tile_col) * TILE + at_row - at_col >= 0
                    keep = inner | ((tile_row == tile_col) & (tile_col >= PANELS))
                out_ref[down, across] = jnp.where(keep, value, 0.0)
        if reach < tile_cols:
            out_ref[:, reach * TILE :] = jnp.zeros((rows_here, cols_count - reach * TILE), jnp.float32)

    for at in range(pl.num_programs(0)):
        pl.when(step == at)(lambda at=at: rows_of(at))


def trailing(grid_rows, grid_cols, place, matrix, lower, cols, inverse):
    rows_count, cols_count = matrix.shape
    rows_step = 2 * TILE
    return pl.pallas_call(
        functools.partial(trailing_kernel, grid_rows, grid_cols),
        grid=(rows_count // rows_step,),
        out_shape=jax.ShapeDtypeStruct(matrix.shape, jnp.float32),
        in_specs=[
            pl.BlockSpec(memory_space=pltpu.SMEM),
            pl.BlockSpec((rows_step, cols_count), lambda t: (t, 0)),
            pl.BlockSpec((rows_step, WIDTH), lambda t: (t, 0)),
            pl.BlockSpec(cols.shape, lambda t: (0, 0, 0, 0, 0)),
            pl.BlockSpec(inverse.shape, lambda t: (0, 0)),
        ],
        out_specs=pl.BlockSpec((rows_step, cols_count), lambda t: (t, 0)),
        scratch_shapes=[pltpu.VMEM((cols_count, 3 * WIDTH), jnp.bfloat16)],
        name="trailing",
    )(place, matrix, lower, cols, inverse)


def exchange(chunks, axis):
    return lax.all_to_all(chunks, axis, 0, 0, tiled=True)


def to_all(part, axis):
    count = lax.axis_size(axis)
    return exchange(jnp.broadcast_to(part[None], (count, *part.shape)), axis)


def on_device(matrix):
    rows_count, cols_count = matrix.shape
    grid_rows = lax.axis_size("row")
    grid_cols = lax.axis_size("col")
    chips = grid_cols // PANELS
    tile_rows, tile_cols = rows_count // TILE, cols_count // TILE
    wraps = grid_cols // grid_rows
    place = jnp.stack([lax.axis_index("row"), lax.axis_index("col")]).astype(jnp.int32)
    with jax.named_scope("scatter_rows"):
        panel = matrix[:, :TILE].reshape(tile_rows, chips, GROUP, TILE).transpose(1, 0, 2, 3)
        same_core = [list(range(p, grid_cols, PANELS)) for p in range(PANELS)]
        piece = lax.all_to_all(panel, "col", 0, 0, tiled=True, axis_index_groups=same_core)[0]
        piece, place = lax.optimization_barrier((piece, place))
    with jax.named_scope("gather_rows"):
        held = to_all(piece, "col")
    with jax.named_scope("gather_planes"):
        planes = lax.all_gather(piece, "row")
        held, planes = lax.optimization_barrier((held, planes))
    with jax.named_scope("spread_diagonal"):
        diag = to_all(planes[:PANELS, 0], "col")
    with jax.named_scope("exchange_cols"):
        diag, planes = lax.optimization_barrier((diag, planes))
        parts = planes.reshape(grid_rows, tile_cols, wraps, GROUP, TILE).transpose(2, 0, 1, 3, 4)
        cols = exchange(parts.reshape(grid_cols, tile_cols, GROUP, TILE), "col")
    inverse, lower = panels(
        diag.reshape(chips, PANELS, *diag.shape[1:]), held.reshape(chips, PANELS, *held.shape[1:])
    )
    cols = cols.reshape(chips, PANELS, *cols.shape[1:])
    return trailing(grid_rows, grid_cols, place, matrix, lower, cols, inverse)


def solution(mesh):
    return jax.shard_map(
        on_device, mesh=mesh, in_specs=(P("row", "col"),), out_specs=P("row", "col"), check_vma=False
    )
```

```python
import functools

import jax
import jax.numpy as jnp
from jax import lax
from jax.experimental import pallas as pl
from jax.experimental.pallas import tpu as pltpu
from jax.sharding import PartitionSpec as P

TILE = 128
PANELS = 2
WIDTH = TILE * PANELS
STRIP = 64
GROUP = 8
STEP = 2
HIGHEST = lax.Precision.HIGHEST


def product(lhs, rhs, contract):
    return lax.dot_general(
        lhs, rhs, (contract, ((), ())), precision=HIGHEST, preferred_element_type=jnp.float32
    )


def split(value):
    high = value.astype(jnp.bfloat16)
    return high, (value - high.astype(jnp.float32)).astype(jnp.bfloat16)


def eliminate(strip, pivot_lane):
    count, width = strip.shape
    shape = (GROUP, TILE)
    tiles = [
        [strip[t * GROUP : (t + 1) * GROUP, v * TILE : (v + 1) * TILE] for v in range(width // TILE)]
        for t in range(count // GROUP)
    ]
    sub_row = lax.broadcasted_iota(jnp.int32, shape, 0)

    def over_lanes(tile, lane):
        return jnp.broadcast_to(tile[:, lane : lane + 1], shape)

    def over_rows(tile, row):
        return jnp.broadcast_to(tile[row : row + 1], shape)

    scaled = []
    for own in range(len(tiles)):
        block, lane = divmod(pivot_lane + GROUP * own, TILE)
        columns = [
            [over_lanes(parts[block], lane + k) for k in range(GROUP)] for parts in tiles[own:]
        ]
        pivots = jnp.ones(shape, jnp.float32)
        for k in range(GROUP):
            pivot_row = {j: over_rows(columns[0][j], k) for j in range(k, GROUP)}
            inverse = 1.0 / pivot_row[k]
            pivots = jnp.where(sub_row == k, pivot_row[k], pivots)
            rows = [over_rows(part, k) for part in tiles[own]]
            for t, column in enumerate(columns, own):
                factor = column[k] * inverse
                for j in range(k + 1, GROUP):
                    column[j] = column[j] - factor * pivot_row[j]
                if t == own:
                    factor = jnp.where(sub_row > k, factor, 0.0)
                tiles[t] = [part - factor * row for part, row in zip(tiles[t], rows)]
        scale = lax.rsqrt(pivots)
        scaled.append(jnp.concatenate([part * scale for part in tiles[own]], axis=1))
    return jnp.concatenate(scaled, axis=0)


def panels_kernel(
    wraps, diag_ref, held_ref, inverse_ref, lower_hbm_ref, work_ref, raw_ref, lower_ref, sems
):
    fetch = pltpu.make_async_copy(held_ref, raw_ref, sems.at[0])
    fetch.start()
    for p in range(PANELS):
        for q in range(PANELS):
            part = diag_ref[:, q, p].reshape(TILE, TILE)
            work_ref[p * TILE : (p + 1) * TILE, q * TILE : (q + 1) * TILE] = part
    at_row = lax.broadcasted_iota(jnp.int32, (WIDTH, WIDTH), 0)
    at_col = lax.broadcasted_iota(jnp.int32, (WIDTH, WIDTH), 1)
    inverse_ref[...] = jnp.where(at_row == at_col, 1.0, 0.0).astype(jnp.float32)
    tile_rows = lower_ref.shape[0] // TILE
    sends = []
    order = [t % wraps * (tile_rows // wraps) + t // wraps for t in range(tile_rows)]
    for start in range(0, WIDTH, STRIP):
        stop = start + STRIP
        first = start // TILE * TILE
        upper = WIDTH - first
        done = first + TILE
        strip = jnp.concatenate(
            [work_ref[start:stop, first:], inverse_ref[start:stop, :done]], axis=1
        )
        strip = eliminate(strip, start - first)
        inverse_ref[start:stop, :done] = strip[:, upper:]
        if stop < WIDTH:
            update = product(strip[:, :upper], strip, ((0,), (0,)))[stop - first :]
            work_ref[stop:, first:] = work_ref[stop:, first:] - update[:, :upper]
            inverse_ref[stop:, :done] = inverse_ref[stop:, :done] - update[:, upper:]
        if stop % TILE == 0:
            if first == 0:
                fetch.wait()
            raw = jnp.concatenate(
                [
                    jnp.concatenate(
                        [raw_ref[:, p, at].reshape(TILE, TILE) for at in order], axis=0
                    )
                    for p in range(done // TILE)
                ],
                axis=1,
            )
            lower_ref[:, first:done] = product(raw, inverse_ref[first:done, :done], ((1,), (1,)))
            send = pltpu.make_async_copy(
                lower_ref.at[:, first:done], lower_hbm_ref.at[:, first:done], sems.at[done // TILE]
            )
            send.start()
            sends.append(send)
    for send in sends:
        send.wait()


def in_vmem(*arrays):
    return [pltpu.with_memory_space_constraint(x, pltpu.VMEM) for x in arrays]


def panels(wraps, diag, held):
    count = held.shape[0] * held.shape[2] * GROUP
    vmem = pl.BlockSpec(memory_space=pltpu.VMEM)
    return pl.pallas_call(
        functools.partial(panels_kernel, wraps),
        out_shape=[
            pltpu.VMEM((WIDTH, WIDTH), jnp.float32),
            pltpu.HBM((count, WIDTH), jnp.float32),
        ],
        in_specs=[vmem, pl.BlockSpec(memory_space=pltpu.HBM)],
        out_specs=[vmem, pl.BlockSpec(memory_space=pltpu.HBM)],
        scratch_shapes=[
            pltpu.VMEM((WIDTH, WIDTH), jnp.float32),
            pltpu.VMEM(held.shape, jnp.float32),
            pltpu.VMEM((count, WIDTH), jnp.float32),
            pltpu.SemaphoreType.DMA((1 + PANELS,)),
        ],
        cost_estimate=pl.CostEstimate(
            flops=4 * WIDTH**3 + 12 * count * WIDTH**2,
            bytes_accessed=12 * WIDTH**2 + 8 * count * WIDTH,
            transcendentals=0,
        ),
        compiler_params=pltpu.CompilerParams(vmem_limit_bytes=32 * 2**20),
        name="panels",
    )(*in_vmem(diag), pltpu.with_memory_space_constraint(held, pltpu.HBM))


def trailing_kernel(
    grid_rows, grid_cols, place_ref, matrix_ref, lower_hbm_ref, cols_ref, inverse_ref, out_ref, lower_ref, done_ref, sems
):
    fetch = pltpu.make_async_copy(lower_hbm_ref, lower_ref, sems.at[0])
    fetch.start()
    row_index, col_index = place_ref[0], place_ref[1]
    rows_count, cols_count = matrix_ref.shape
    tile_rows, tile_cols = rows_count // TILE, cols_count // TILE
    raw = jnp.concatenate(
        [
            jnp.concatenate(
                [
                    cols_ref[:, p, wrap, b].reshape(-1, TILE)
                    for b in range(tile_cols)
                    for wrap in range(cols_ref.shape[2])
                ],
                axis=0,
            )
            for p in range(PANELS)
        ],
        axis=1,
    )
    high, low = split(product(raw, inverse_ref[...], ((1,), (1,))))
    solved = jnp.concatenate([high, low, high], axis=1)
    fetch.wait()
    at_row = lax.broadcasted_iota(jnp.int32, (TILE, TILE), 0)
    at_col = lax.broadcasted_iota(jnp.int32, (TILE, TILE), 1)
    sends = []
    for step in reversed(range(tile_rows // STEP)):
        span = slice(step * STEP * TILE, (step + 1) * STEP * TILE)
        last_tile_row = ((step + 1) * STEP - 1) * grid_rows + grid_rows - 1
        reach = min(tile_cols, last_tile_row // grid_cols + 1)
        high, low = split(lower_ref[span, :])
        update = lax.dot_general(
            jnp.concatenate([high, high, low], axis=1),
            solved[: reach * TILE],
            (((1,), (1,)), ((), ())),
            preferred_element_type=jnp.float32,
        )
        for t in range(STEP):
            tile_row = (step * STEP + t) * grid_rows + row_index
            down = slice((step * STEP + t) * TILE, (step * STEP + t + 1) * TILE)
            for b in range(reach):
                across = slice(b * TILE, (b + 1) * TILE)
                tile_col = b * grid_cols + col_index
                value = matrix_ref[down, across] - update[t * TILE : (t + 1) * TILE, across]
                keep = tile_row >= tile_col
                if b * grid_cols < PANELS:
                    for p in range(PANELS):
                        panel = lower_ref[down, p * TILE : (p + 1) * TILE]
                        value = jnp.where(tile_col == p, panel, value)
                    inner = (tile_row - tile_col) * TILE + at_row - at_col >= 0
                    keep = inner | ((tile_row == tile_col) & (tile_col >= PANELS))
                done_ref[down, across] = jnp.where(keep, value, 0.0)
        if reach < tile_cols:
            beyond = slice(reach * TILE, cols_count)
            done_ref[span, beyond] = jnp.zeros((STEP * TILE, cols_count - reach * TILE), jnp.float32)
        send = pltpu.make_async_copy(done_ref.at[span], out_ref.at[span], sems.at[step + 1])
        send.start()
        sends.append(send)
    for send in sends:
        send.wait()


def trailing(grid_rows, grid_cols, place, matrix, lower, cols, inverse):
    vmem = pl.BlockSpec(memory_space=pltpu.VMEM)
    matrix, cols, inverse = in_vmem(matrix, cols, inverse)
    lower = pltpu.with_memory_space_constraint(lower, pltpu.HBM)
    return pl.pallas_call(
        functools.partial(trailing_kernel, grid_rows, grid_cols),
        out_shape=jax.ShapeDtypeStruct(matrix.shape, jnp.float32),
        in_specs=[
            pl.BlockSpec(memory_space=pltpu.SMEM),
            vmem,
            pl.BlockSpec(memory_space=pltpu.HBM),
            vmem,
            vmem,
        ],
        out_specs=pl.BlockSpec(memory_space=pl.ANY),
        scratch_shapes=[
            pltpu.VMEM(lower.shape, jnp.float32),
            pltpu.VMEM(matrix.shape, jnp.float32),
            pltpu.SemaphoreType.DMA((matrix.shape[0] // (STEP * TILE) + 1,)),
        ],
        compiler_params=pltpu.CompilerParams(vmem_limit_bytes=32 * 2**20),
        name="trailing",
    )(place, matrix, lower, cols, inverse)


def exchange(chunks, axis):
    return lax.all_to_all(chunks, axis, 0, 0, tiled=True)


def to_all(part, axis):
    count = lax.axis_size(axis)
    return exchange(jnp.broadcast_to(part[None], (count, *part.shape)), axis)


def on_device(matrix):
    rows_count, cols_count = matrix.shape
    grid_rows = lax.axis_size("row")
    grid_cols = lax.axis_size("col")
    chips = grid_cols // PANELS
    tile_cols = cols_count // TILE
    wraps = grid_cols // grid_rows
    place = jnp.stack([lax.axis_index("row"), lax.axis_index("col")]).astype(jnp.int32)
    with jax.named_scope("scatter_rows"):
        panel = matrix[:, :TILE].reshape(tile_cols, wraps, chips, GROUP, TILE)
        panel = panel.transpose(2, 1, 0, 3, 4).reshape(chips, wraps * tile_cols, GROUP, TILE)
        same_core = [list(range(p, grid_cols, PANELS)) for p in range(PANELS)]
        piece = lax.all_to_all(panel, "col", 0, 0, tiled=True, axis_index_groups=same_core)[0]
    with jax.named_scope("gather_rows"):
        held = to_all(piece, "col")
    with jax.named_scope("gather_planes"):
        planes = lax.all_gather(piece, "row")
        held, planes = lax.optimization_barrier((held, planes))
    with jax.named_scope("spread_diagonal"):
        diag = to_all(planes[:PANELS, 0], "col")
    with jax.named_scope("exchange_cols"):
        diag, planes = lax.optimization_barrier((diag, planes))
        parts = planes.reshape(grid_cols, tile_cols, GROUP, TILE)
        by_plane = [w * grid_rows + q for q in range(grid_rows) for w in range(wraps)]
        cols = lax.all_to_all(parts, "col", 0, 0, tiled=True, axis_index_groups=[by_plane])
        cols = cols.reshape(grid_rows // PANELS, PANELS, wraps, *cols.shape[1:])
    inverse, lower = panels(
        wraps,
        diag.reshape(chips, PANELS, *diag.shape[1:]),
        held.reshape(chips, PANELS, *held.shape[1:]),
    )
    return trailing(grid_rows, grid_cols, place, matrix, lower, cols, inverse)


def solution(mesh):
    return jax.shard_map(
        on_device, mesh=mesh, in_specs=(P("row", "col"),), out_specs=P("row", "col"), check_vma=False
    )
```

```python
import functools

import jax
import jax.numpy as jnp
from jax import lax
from jax.experimental import pallas as pl
from jax.experimental.pallas import tpu as pltpu
from jax.sharding import PartitionSpec as P

TILE = 128
PANELS = 2
WIDTH = TILE * PANELS
STRIP = 64
GROUP = 8
STEP = 2
HIGHEST = lax.Precision.HIGHEST


def product(lhs, rhs, contract):
    return lax.dot_general(
        lhs, rhs, (contract, ((), ())), precision=HIGHEST, preferred_element_type=jnp.float32
    )


def split(value):
    high = value.astype(jnp.bfloat16)
    return high, (value - high.astype(jnp.float32)).astype(jnp.bfloat16)


def eliminate(strip, pivot_lane):
    count, width = strip.shape
    shape = (GROUP, TILE)
    tiles = [
        [strip[t * GROUP : (t + 1) * GROUP, v * TILE : (v + 1) * TILE] for v in range(width // TILE)]
        for t in range(count // GROUP)
    ]
    sub_row = lax.broadcasted_iota(jnp.int32, shape, 0)

    def over_lanes(tile, lane):
        return jnp.broadcast_to(tile[:, lane : lane + 1], shape)

    def over_rows(tile, row):
        return jnp.broadcast_to(tile[row : row + 1], shape)

    scaled = []
    for own in range(len(tiles)):
        block, lane = divmod(pivot_lane + GROUP * own, TILE)
        columns = [
            [over_lanes(parts[block], lane + k) for k in range(GROUP)] for parts in tiles[own:]
        ]
        pivots = jnp.ones(shape, jnp.float32)
        for k in range(GROUP):
            pivot_row = {j: over_rows(columns[0][j], k) for j in range(k, GROUP)}
            inverse = 1.0 / pivot_row[k]
            pivots = jnp.where(sub_row == k, pivot_row[k], pivots)
            rows = [over_rows(part, k) for part in tiles[own]]
            for t, column in enumerate(columns, own):
                factor = column[k] * inverse
                for j in range(k + 1, GROUP):
                    column[j] = column[j] - factor * pivot_row[j]
                if t == own:
                    factor = jnp.where(sub_row > k, factor, 0.0)
                tiles[t] = [part - factor * row for part, row in zip(tiles[t], rows)]
        scale = lax.rsqrt(pivots)
        scaled.append(jnp.concatenate([part * scale for part in tiles[own]], axis=1))
    return jnp.concatenate(scaled, axis=0)


def panels_kernel(
    wraps, place_ref, diag_ref, own_ref, other_ref, inverse_ref, lower_hbm_ref, work_ref, raw_ref, lower_ref, sems
):
    core = lax.rem(place_ref[1], PANELS)
    fetches = [
        pltpu.make_async_copy(own_ref, raw_ref.at[core], sems.at[PANELS]),
        pltpu.make_async_copy(other_ref, raw_ref.at[PANELS - 1 - core], sems.at[PANELS + 1]),
    ]
    for fetch in fetches:
        fetch.start()
    for p in range(PANELS):
        for q in range(PANELS):
            part = diag_ref[:, q, p].reshape(TILE, TILE)
            work_ref[p * TILE : (p + 1) * TILE, q * TILE : (q + 1) * TILE] = part
    at_row = lax.broadcasted_iota(jnp.int32, (WIDTH, WIDTH), 0)
    at_col = lax.broadcasted_iota(jnp.int32, (WIDTH, WIDTH), 1)
    inverse_ref[...] = jnp.where(at_row == at_col, 1.0, 0.0).astype(jnp.float32)
    tile_rows = lower_ref.shape[0] // TILE
    sends = []
    order = [t % wraps * (tile_rows // wraps) + t // wraps for t in range(tile_rows)]
    for start in range(0, WIDTH, STRIP):
        stop = start + STRIP
        first = start // TILE * TILE
        upper = WIDTH - first
        done = first + TILE
        strip = jnp.concatenate(
            [work_ref[start:stop, first:], inverse_ref[start:stop, :done]], axis=1
        )
        strip = eliminate(strip, start - first)
        inverse_ref[start:stop, :done] = strip[:, upper:]
        if stop < WIDTH:
            update = product(strip[:, :upper], strip, ((0,), (0,)))[stop - first :]
            work_ref[stop:, first:] = work_ref[stop:, first:] - update[:, :upper]
            inverse_ref[stop:, :done] = inverse_ref[stop:, :done] - update[:, upper:]
        if stop % TILE == 0:
            if first == 0:
                for fetch in fetches:
                    fetch.wait()
            raw = jnp.concatenate(
                [
                    jnp.concatenate(
                        [raw_ref[p, :, at].reshape(TILE, TILE) for at in order], axis=0
                    )
                    for p in range(done // TILE)
                ],
                axis=1,
            )
            lower_ref[:, first:done] = product(raw, inverse_ref[first:done, :done], ((1,), (1,)))
            send = pltpu.make_async_copy(
                lower_ref.at[:, first:done], lower_hbm_ref.at[:, first:done], sems.at[first // TILE]
            )
            send.start()
            sends.append(send)
    for send in sends:
        send.wait()


def in_vmem(*arrays):
    return [pltpu.with_memory_space_constraint(x, pltpu.VMEM) for x in arrays]


def in_hbm(*arrays):
    return [pltpu.with_memory_space_constraint(x, pltpu.HBM) for x in arrays]


def panels(wraps, place, diag, own, other):
    count = own.shape[0] * own.shape[1] * GROUP
    hbm = pl.BlockSpec(memory_space=pltpu.HBM)
    vmem = pl.BlockSpec(memory_space=pltpu.VMEM)
    return pl.pallas_call(
        functools.partial(panels_kernel, wraps),
        out_shape=[
            pltpu.VMEM((WIDTH, WIDTH), jnp.float32),
            pltpu.HBM((count, WIDTH), jnp.float32),
        ],
        in_specs=[pl.BlockSpec(memory_space=pltpu.SMEM), vmem, hbm, hbm],
        out_specs=[vmem, hbm],
        scratch_shapes=[
            pltpu.VMEM((WIDTH, WIDTH), jnp.float32),
            pltpu.VMEM((PANELS, *own.shape), jnp.float32),
            pltpu.VMEM((count, WIDTH), jnp.float32),
            pltpu.SemaphoreType.DMA((2 * PANELS,)),
        ],
        cost_estimate=pl.CostEstimate(
            flops=4 * WIDTH**3 + 12 * count * WIDTH**2,
            bytes_accessed=12 * WIDTH**2 + 8 * count * WIDTH,
            transcendentals=0,
        ),
        compiler_params=pltpu.CompilerParams(vmem_limit_bytes=32 * 2**20),
        name="panels",
    )(place, *in_vmem(diag), *in_hbm(own, other))


def trailing_kernel(
    grid_rows, grid_cols, place_ref, matrix_ref, lower_hbm_ref, cols_ref, inverse_ref, out_ref, lower_ref, done_ref, sems
):
    fetch = pltpu.make_async_copy(lower_hbm_ref, lower_ref, sems.at[0])
    fetch.start()
    row_index, col_index = place_ref[0], place_ref[1]
    rows_count, cols_count = matrix_ref.shape
    tile_rows, tile_cols = rows_count // TILE, cols_count // TILE
    raw = jnp.concatenate(
        [
            jnp.concatenate(
                [
                    cols_ref[:, p, wrap, b].reshape(-1, TILE)
                    for b in range(tile_cols)
                    for wrap in range(cols_ref.shape[2])
                ],
                axis=0,
            )
            for p in range(PANELS)
        ],
        axis=1,
    )
    high, low = split(product(raw, inverse_ref[...], ((1,), (1,))))
    solved = jnp.concatenate([high, low, high], axis=1)
    fetch.wait()
    at_row = lax.broadcasted_iota(jnp.int32, (TILE, TILE), 0)
    at_col = lax.broadcasted_iota(jnp.int32, (TILE, TILE), 1)
    sends = []
    for step in reversed(range(tile_rows // STEP)):
        span = slice(step * STEP * TILE, (step + 1) * STEP * TILE)
        last_tile_row = ((step + 1) * STEP - 1) * grid_rows + grid_rows - 1
        reach = min(tile_cols, last_tile_row // grid_cols + 1)
        high, low = split(lower_ref[span, :])
        update = lax.dot_general(
            jnp.concatenate([high, high, low], axis=1),
            solved[: reach * TILE],
            (((1,), (1,)), ((), ())),
            preferred_element_type=jnp.float32,
        )
        for t in range(STEP):
            tile_row = (step * STEP + t) * grid_rows + row_index
            down = slice((step * STEP + t) * TILE, (step * STEP + t + 1) * TILE)
            for b in range(reach):
                across = slice(b * TILE, (b + 1) * TILE)
                tile_col = b * grid_cols + col_index
                value = matrix_ref[down, across] - update[t * TILE : (t + 1) * TILE, across]
                keep = tile_row >= tile_col
                if b * grid_cols < PANELS:
                    for p in range(PANELS):
                        panel = lower_ref[down, p * TILE : (p + 1) * TILE]
                        value = jnp.where(tile_col == p, panel, value)
                    inner = (tile_row - tile_col) * TILE + at_row - at_col >= 0
                    keep = inner | ((tile_row == tile_col) & (tile_col >= PANELS))
                done_ref[down, across] = jnp.where(keep, value, 0.0)
        if reach < tile_cols:
            beyond = slice(reach * TILE, cols_count)
            done_ref[span, beyond] = jnp.zeros((STEP * TILE, cols_count - reach * TILE), jnp.float32)
        send = pltpu.make_async_copy(done_ref.at[span], out_ref.at[span], sems.at[step + 1])
        send.start()
        sends.append(send)
    for send in sends:
        send.wait()


def trailing(grid_rows, grid_cols, place, matrix, lower, cols, inverse):
    vmem = pl.BlockSpec(memory_space=pltpu.VMEM)
    matrix, cols, inverse = in_vmem(matrix, cols, inverse)
    (lower,) = in_hbm(lower)
    return pl.pallas_call(
        functools.partial(trailing_kernel, grid_rows, grid_cols),
        out_shape=jax.ShapeDtypeStruct(matrix.shape, jnp.float32),
        in_specs=[
            pl.BlockSpec(memory_space=pltpu.SMEM),
            vmem,
            pl.BlockSpec(memory_space=pltpu.HBM),
            vmem,
            vmem,
        ],
        out_specs=pl.BlockSpec(memory_space=pl.ANY),
        scratch_shapes=[
            pltpu.VMEM(lower.shape, jnp.float32),
            pltpu.VMEM(matrix.shape, jnp.float32),
            pltpu.SemaphoreType.DMA((matrix.shape[0] // (STEP * TILE) + 1,)),
        ],
        compiler_params=pltpu.CompilerParams(vmem_limit_bytes=32 * 2**20),
        name="trailing",
    )(place, matrix, lower, cols, inverse)


def exchange(chunks, axis):
    return lax.all_to_all(chunks, axis, 0, 0, tiled=True)


def to_all(part, axis):
    count = lax.axis_size(axis)
    return exchange(jnp.broadcast_to(part[None], (count, *part.shape)), axis)


def on_device(matrix):
    rows_count, cols_count = matrix.shape
    grid_rows = lax.axis_size("row")
    grid_cols = lax.axis_size("col")
    chips = grid_cols // PANELS
    tile_cols = cols_count // TILE
    wraps = grid_cols // grid_rows
    place = jnp.stack([lax.axis_index("row"), lax.axis_index("col")]).astype(jnp.int32)
    with jax.named_scope("scatter_rows"):
        panel = matrix[:, :TILE].reshape(tile_cols, wraps, chips, GROUP, TILE)
        panel = panel.transpose(2, 1, 0, 3, 4).reshape(chips, wraps * tile_cols, GROUP, TILE)
        same_core = [list(range(p, grid_cols, PANELS)) for p in range(PANELS)]
        piece = lax.all_to_all(panel, "col", 0, 0, tiled=True, axis_index_groups=same_core)[0]
    with jax.named_scope("gather_rows"):
        copies = jnp.broadcast_to(piece[None], (chips, *piece.shape))
        own = lax.all_to_all(copies, "col", 0, 0, tiled=True, axis_index_groups=same_core)
    with jax.named_scope("gather_planes"):
        planes = lax.all_gather(piece, "row", tiled=True)
        own, planes = lax.optimization_barrier((own, planes))
        planes = planes.reshape(grid_rows, *piece.shape)
    with jax.named_scope("swap_panels"):
        other = lax.ppermute(own, "col", [(c, c ^ 1) for c in range(grid_cols)])
    with jax.named_scope("spread_diagonal"):
        diag = to_all(planes[:PANELS, 0], "col")
    with jax.named_scope("exchange_cols"):
        diag, planes = lax.optimization_barrier((diag, planes))
        parts = planes.reshape(grid_rows, wraps, tile_cols, GROUP, TILE).swapaxes(0, 1)
        cols = exchange(parts.reshape(grid_cols, tile_cols, GROUP, TILE), "col")
        cols = cols.reshape(chips, PANELS, 1, *cols.shape[1:])
    diag = diag.reshape(chips, PANELS, *diag.shape[1:])
    inverse, lower = panels(wraps, place, diag, own, other)
    return trailing(grid_rows, grid_cols, place, matrix, lower, cols, inverse)


def solution(mesh):
    return jax.shard_map(
        on_device, mesh=mesh, in_specs=(P("row", "col"),), out_specs=P("row", "col"), check_vma=False
    )
```

```python
import functools

import jax
import jax.numpy as jnp
from jax import lax
from jax.experimental import pallas as pl
from jax.experimental.pallas import tpu as pltpu
from jax.sharding import PartitionSpec as P

TILE = 128
PANELS = 2
WIDTH = TILE * PANELS
STRIP = 64
GROUP = 8
STEP = 2
HIGHEST = lax.Precision.HIGHEST


def product(lhs, rhs, contract):
    return lax.dot_general(
        lhs, rhs, (contract, ((), ())), precision=HIGHEST, preferred_element_type=jnp.float32
    )


def split(value):
    high = value.astype(jnp.bfloat16)
    return high, (value - high.astype(jnp.float32)).astype(jnp.bfloat16)


def eliminate(strip, pivot_lane):
    count, width = strip.shape
    shape = (GROUP, TILE)
    tiles = [
        [strip[t * GROUP : (t + 1) * GROUP, v * TILE : (v + 1) * TILE] for v in range(width // TILE)]
        for t in range(count // GROUP)
    ]
    sub_row = lax.broadcasted_iota(jnp.int32, shape, 0)

    def over_lanes(tile, lane):
        return [jnp.broadcast_to(tile[:, lane + k : lane + k + 1], shape) for k in range(GROUP)]

    def over_rows(tile, row):
        return jnp.broadcast_to(tile[row : row + 1], shape)

    scaled = []
    carried = None
    for own in range(len(tiles)):
        block, lane = divmod(pivot_lane + GROUP * own, TILE)
        columns = [over_lanes(parts[block], lane) for parts in tiles[own + 1 :]]
        columns.insert(0, carried or over_lanes(tiles[own][block], lane))
        ahead = own + 1 < len(tiles) and lane + GROUP < TILE
        carried = None
        if ahead:
            beside = over_lanes(tiles[own][block], lane + GROUP)
            carried = over_lanes(tiles[own + 1][block], lane + GROUP)
        pivots = jnp.ones(shape, jnp.float32)
        for k in range(GROUP):
            pivot_row = {j: over_rows(columns[0][j], k) for j in range(k, GROUP)}
            inverse = 1.0 / pivot_row[k]
            pivots = jnp.where(sub_row == k, pivot_row[k], pivots)
            rows = [over_rows(part, k) for part in tiles[own]]
            if ahead:
                beside_row = [over_rows(column, k) for column in beside]
            for t, column in enumerate(columns, own):
                factor = column[k] * inverse
                for j in range(k + 1, GROUP):
                    column[j] = column[j] - factor * pivot_row[j]
                if ahead and t == own:
                    beside = [kept - factor * row for kept, row in zip(beside, beside_row)]
                if ahead and t == own + 1:
                    carried = [kept - factor * row for kept, row in zip(carried, beside_row)]
                if t == own:
                    factor = jnp.where(sub_row > k, factor, 0.0)
                tiles[t] = [part - factor * row for part, row in zip(tiles[t], rows)]
        scale = lax.rsqrt(pivots)
        scaled.append(jnp.concatenate([part * scale for part in tiles[own]], axis=1))
    return jnp.concatenate(scaled, axis=0)


def panels_kernel(
    wraps, place_ref, diag_ref, own_ref, other_ref, inverse_ref, lower_hbm_ref, work_ref, raw_ref, lower_ref, sems
):
    core = lax.rem(place_ref[1], PANELS)
    fetches = [
        pltpu.make_async_copy(own_ref, raw_ref.at[core], sems.at[PANELS]),
        pltpu.make_async_copy(other_ref, raw_ref.at[PANELS - 1 - core], sems.at[PANELS + 1]),
    ]
    for fetch in fetches:
        fetch.start()
    for p in range(PANELS):
        for q in range(PANELS):
            part = diag_ref[:, q, p].reshape(TILE, TILE)
            work_ref[p * TILE : (p + 1) * TILE, q * TILE : (q + 1) * TILE] = part
    at_row = lax.broadcasted_iota(jnp.int32, (WIDTH, WIDTH), 0)
    at_col = lax.broadcasted_iota(jnp.int32, (WIDTH, WIDTH), 1)
    inverse_ref[...] = jnp.where(at_row == at_col, 1.0, 0.0).astype(jnp.float32)
    tile_rows = lower_ref.shape[0] // TILE
    sends = []
    order = [t % wraps * (tile_rows // wraps) + t // wraps for t in range(tile_rows)]
    for start in range(0, WIDTH, STRIP):
        stop = start + STRIP
        first = start // TILE * TILE
        upper = WIDTH - first
        done = first + TILE
        strip = jnp.concatenate(
            [work_ref[start:stop, first:], inverse_ref[start:stop, :done]], axis=1
        )
        strip = eliminate(strip, start - first)
        inverse_ref[start:stop, :done] = strip[:, upper:]
        if stop < WIDTH:
            update = product(strip[:, :upper], strip, ((0,), (0,)))[stop - first :]
            work_ref[stop:, first:] = work_ref[stop:, first:] - update[:, :upper]
            inverse_ref[stop:, :done] = inverse_ref[stop:, :done] - update[:, upper:]
        if stop % TILE == 0:
            if first == 0:
                for fetch in fetches:
                    fetch.wait()
            raw = jnp.concatenate(
                [
                    jnp.concatenate(
                        [raw_ref[p, :, at].reshape(TILE, TILE) for at in order], axis=0
                    )
                    for p in range(done // TILE)
                ],
                axis=1,
            )
            lower_ref[:, first:done] = product(raw, inverse_ref[first:done, :done], ((1,), (1,)))
            send = pltpu.make_async_copy(
                lower_ref.at[:, first:done], lower_hbm_ref.at[:, first:done], sems.at[first // TILE]
            )
            send.start()
            sends.append(send)
    for send in sends:
        send.wait()


def in_vmem(*arrays):
    return [pltpu.with_memory_space_constraint(x, pltpu.VMEM) for x in arrays]


def in_hbm(*arrays):
    return [pltpu.with_memory_space_constraint(x, pltpu.HBM) for x in arrays]


def panels(wraps, place, diag, own, other):
    count = own.shape[0] * own.shape[1] * GROUP
    hbm = pl.BlockSpec(memory_space=pltpu.HBM)
    vmem = pl.BlockSpec(memory_space=pltpu.VMEM)
    return pl.pallas_call(
        functools.partial(panels_kernel, wraps),
        out_shape=[
            pltpu.VMEM((WIDTH, WIDTH), jnp.float32),
            pltpu.HBM((count, WIDTH), jnp.float32),
        ],
        in_specs=[pl.BlockSpec(memory_space=pltpu.SMEM), vmem, hbm, hbm],
        out_specs=[vmem, hbm],
        scratch_shapes=[
            pltpu.VMEM((WIDTH, WIDTH), jnp.float32),
            pltpu.VMEM((PANELS, *own.shape), jnp.float32),
            pltpu.VMEM((count, WIDTH), jnp.float32),
            pltpu.SemaphoreType.DMA((2 * PANELS,)),
        ],
        cost_estimate=pl.CostEstimate(
            flops=4 * WIDTH**3 + 12 * count * WIDTH**2,
            bytes_accessed=12 * WIDTH**2 + 8 * count * WIDTH,
            transcendentals=0,
        ),
        compiler_params=pltpu.CompilerParams(vmem_limit_bytes=32 * 2**20),
        name="panels",
    )(place, *in_vmem(diag), *in_hbm(own, other))


def trailing_kernel(
    grid_rows, grid_cols, place_ref, matrix_ref, lower_hbm_ref, cols_ref, inverse_ref, out_ref, lower_ref, done_ref, sems
):
    fetch = pltpu.make_async_copy(lower_hbm_ref, lower_ref, sems.at[0])
    fetch.start()
    row_index, col_index = place_ref[0], place_ref[1]
    rows_count, cols_count = matrix_ref.shape
    tile_rows, tile_cols = rows_count // TILE, cols_count // TILE
    raw = jnp.concatenate(
        [
            jnp.concatenate(
                [
                    cols_ref[:, p, wrap, b].reshape(-1, TILE)
                    for b in range(tile_cols)
                    for wrap in range(cols_ref.shape[2])
                ],
                axis=0,
            )
            for p in range(PANELS)
        ],
        axis=1,
    )
    high, low = split(product(raw, inverse_ref[...], ((1,), (1,))))
    solved = jnp.concatenate([high, low, high], axis=1)
    fetch.wait()
    at_row = lax.broadcasted_iota(jnp.int32, (TILE, TILE), 0)
    at_col = lax.broadcasted_iota(jnp.int32, (TILE, TILE), 1)
    sends = []
    for step in reversed(range(tile_rows // STEP)):
        span = slice(step * STEP * TILE, (step + 1) * STEP * TILE)
        last_tile_row = ((step + 1) * STEP - 1) * grid_rows + grid_rows - 1
        reach = min(tile_cols, last_tile_row // grid_cols + 1)
        high, low = split(lower_ref[span, :])
        update = lax.dot_general(
            jnp.concatenate([high, high, low], axis=1),
            solved[: reach * TILE],
            (((1,), (1,)), ((), ())),
            preferred_element_type=jnp.float32,
        )
        for t in range(STEP):
            tile_row = (step * STEP + t) * grid_rows + row_index
            down = slice((step * STEP + t) * TILE, (step * STEP + t + 1) * TILE)
            for b in range(reach):
                across = slice(b * TILE, (b + 1) * TILE)
                tile_col = b * grid_cols + col_index
                value = matrix_ref[down, across] - update[t * TILE : (t + 1) * TILE, across]
                keep = tile_row >= tile_col
                if b * grid_cols < PANELS:
                    for p in range(PANELS):
                        panel = lower_ref[down, p * TILE : (p + 1) * TILE]
                        value = jnp.where(tile_col == p, panel, value)
                    inner = (tile_row - tile_col) * TILE + at_row - at_col >= 0
                    keep = inner | ((tile_row == tile_col) & (tile_col >= PANELS))
                done_ref[down, across] = jnp.where(keep, value, 0.0)
        if reach < tile_cols:
            beyond = slice(reach * TILE, cols_count)
            done_ref[span, beyond] = jnp.zeros((STEP * TILE, cols_count - reach * TILE), jnp.float32)
        send = pltpu.make_async_copy(done_ref.at[span], out_ref.at[span], sems.at[step + 1])
        send.start()
        sends.append(send)
    for send in sends:
        send.wait()


def trailing(grid_rows, grid_cols, place, matrix, lower, cols, inverse):
    vmem = pl.BlockSpec(memory_space=pltpu.VMEM)
    matrix, cols, inverse = in_vmem(matrix, cols, inverse)
    (lower,) = in_hbm(lower)
    return pl.pallas_call(
        functools.partial(trailing_kernel, grid_rows, grid_cols),
        out_shape=jax.ShapeDtypeStruct(matrix.shape, jnp.float32),
        in_specs=[
            pl.BlockSpec(memory_space=pltpu.SMEM),
            vmem,
            pl.BlockSpec(memory_space=pltpu.HBM),
            vmem,
            vmem,
        ],
        out_specs=pl.BlockSpec(memory_space=pl.ANY),
        scratch_shapes=[
            pltpu.VMEM(lower.shape, jnp.float32),
            pltpu.VMEM(matrix.shape, jnp.float32),
            pltpu.SemaphoreType.DMA((matrix.shape[0] // (STEP * TILE) + 1,)),
        ],
        compiler_params=pltpu.CompilerParams(vmem_limit_bytes=32 * 2**20),
        name="trailing",
    )(place, matrix, lower, cols, inverse)


def by_wrap_kernel(planes_ref, parts_ref, sems):
    copies = [
        pltpu.make_async_copy(planes_ref.at[:, w], parts_ref.at[w], sems.at[w])
        for w in range(parts_ref.shape[0])
    ]
    for copy in copies:
        copy.start()
    for copy in copies:
        copy.wait()


def by_wrap(planes):
    count, wraps, *rest = planes.shape
    return pl.pallas_call(
        by_wrap_kernel,
        out_shape=pltpu.HBM((wraps, count, *rest), planes.dtype),
        in_specs=[pl.BlockSpec(memory_space=pltpu.VMEM)],
        out_specs=pl.BlockSpec(memory_space=pltpu.HBM),
        scratch_shapes=[pltpu.SemaphoreType.DMA((wraps,))],
        cost_estimate=pl.CostEstimate(
            flops=0, bytes_accessed=8 * planes.size, transcendentals=0
        ),
        compiler_params=pltpu.CompilerParams(vmem_limit_bytes=2**20),
        name="by_wrap",
    )(*in_vmem(planes))


def exchange(chunks, axis):
    return lax.all_to_all(chunks, axis, 0, 0, tiled=True)


def to_all(part, axis):
    count = lax.axis_size(axis)
    return exchange(jnp.broadcast_to(part[None], (count, *part.shape)), axis)


def on_device(matrix):
    rows_count, cols_count = matrix.shape
    grid_rows = lax.axis_size("row")
    grid_cols = lax.axis_size("col")
    chips = grid_cols // PANELS
    tile_cols = cols_count // TILE
    wraps = grid_cols // grid_rows
    place = jnp.stack([lax.axis_index("row"), lax.axis_index("col")]).astype(jnp.int32)
    with jax.named_scope("scatter_rows"):
        panel = matrix[:, :TILE].reshape(tile_cols, wraps, chips, GROUP, TILE)
        panel = panel.transpose(2, 1, 0, 3, 4).reshape(chips, wraps * tile_cols, GROUP, TILE)
        same_core = [list(range(p, grid_cols, PANELS)) for p in range(PANELS)]
        piece = lax.all_to_all(panel, "col", 0, 0, tiled=True, axis_index_groups=same_core)[0]
    with jax.named_scope("gather_rows"):
        copies = jnp.broadcast_to(piece[None], (chips, *piece.shape))
        own = lax.all_to_all(copies, "col", 0, 0, tiled=True, axis_index_groups=same_core)
    with jax.named_scope("gather_planes"):
        planes = lax.all_gather(piece, "row", tiled=True)
        own, planes = lax.optimization_barrier((own, planes))
        planes = planes.reshape(grid_rows, *piece.shape)
    with jax.named_scope("swap_panels"):
        other = lax.ppermute(own, "col", [(c, c ^ 1) for c in range(grid_cols)])
    with jax.named_scope("spread_diagonal"):
        diag = to_all(planes[:PANELS, 0], "col")
    with jax.named_scope("exchange_cols"):
        parts = by_wrap(planes.reshape(grid_rows, wraps, tile_cols, GROUP, TILE))
        diag, parts = lax.optimization_barrier((diag, parts))
        cols = exchange(parts.reshape(grid_cols, tile_cols, GROUP, TILE), "col")
        cols = cols.reshape(chips, PANELS, 1, *cols.shape[1:])
    diag = diag.reshape(chips, PANELS, *diag.shape[1:])
    inverse, lower = panels(wraps, place, diag, own, other)
    return trailing(grid_rows, grid_cols, place, matrix, lower, cols, inverse)


def solution(mesh):
    return jax.shard_map(
        on_device, mesh=mesh, in_specs=(P("row", "col"),), out_specs=P("row", "col"), check_vma=False
    )
```

```python
import functools

import jax
import jax.numpy as jnp
from jax import lax
from jax.experimental import pallas as pl
from jax.experimental.pallas import tpu as pltpu
from jax.sharding import PartitionSpec as P

TILE = 128
PANELS = 2
WIDTH = TILE * PANELS
STRIP = 64
GROUP = 8
STEP = 2
HIGHEST = lax.Precision.HIGHEST


def product(lhs, rhs, contract):
    return lax.dot_general(
        lhs, rhs, (contract, ((), ())), precision=HIGHEST, preferred_element_type=jnp.float32
    )


def split(value):
    high = value.astype(jnp.bfloat16)
    return high, (value - high.astype(jnp.float32)).astype(jnp.bfloat16)


def eliminate(strip, pivot_lane):
    count, width = strip.shape
    shape = (GROUP, TILE)
    tiles = [
        [strip[t * GROUP : (t + 1) * GROUP, v * TILE : (v + 1) * TILE] for v in range(width // TILE)]
        for t in range(count // GROUP)
    ]
    sub_row = lax.broadcasted_iota(jnp.int32, shape, 0)

    def over_lanes(tile, lane):
        return [jnp.broadcast_to(tile[:, lane + k : lane + k + 1], shape) for k in range(GROUP)]

    def over_rows(tile, row):
        return jnp.broadcast_to(tile[row : row + 1], shape)

    scaled = []
    carried = None
    for own in range(len(tiles)):
        block, lane = divmod(pivot_lane + GROUP * own, TILE)
        columns = [over_lanes(parts[block], lane) for parts in tiles[own + 1 :]]
        columns.insert(0, carried or over_lanes(tiles[own][block], lane))
        ahead = own + 1 < len(tiles) and lane + GROUP < TILE
        carried = None
        if ahead:
            beside = over_lanes(tiles[own][block], lane + GROUP)
            carried = over_lanes(tiles[own + 1][block], lane + GROUP)
        pivots = jnp.ones(shape, jnp.float32)
        for k in range(GROUP):
            pivot_row = {j: over_rows(columns[0][j], k) for j in range(k, GROUP)}
            inverse = 1.0 / pivot_row[k]
            pivots = jnp.where(sub_row == k, pivot_row[k], pivots)
            rows = [over_rows(part, k) for part in tiles[own]]
            if ahead:
                beside_row = [over_rows(column, k) for column in beside]
            for t, column in enumerate(columns, own):
                factor = column[k] * inverse
                for j in range(k + 1, GROUP):
                    column[j] = column[j] - factor * pivot_row[j]
                if ahead and t == own:
                    beside = [kept - factor * row for kept, row in zip(beside, beside_row)]
                if ahead and t == own + 1:
                    carried = [kept - factor * row for kept, row in zip(carried, beside_row)]
                if t == own:
                    factor = jnp.where(sub_row > k, factor, 0.0)
                tiles[t] = [part - factor * row for part, row in zip(tiles[t], rows)]
        scale = lax.rsqrt(pivots)
        scaled.append(jnp.concatenate([part * scale for part in tiles[own]], axis=1))
    return jnp.concatenate(scaled, axis=0)


def panels_kernel(
    wraps, place_ref, diag_ref, own_ref, other_ref, inverse_ref, lower_hbm_ref, work_ref, raw_ref, lower_ref, sems
):
    core = lax.rem(place_ref[1], PANELS)
    fetches = [
        pltpu.make_async_copy(own_ref, raw_ref.at[core], sems.at[PANELS]),
        pltpu.make_async_copy(other_ref, raw_ref.at[PANELS - 1 - core], sems.at[PANELS + 1]),
    ]
    for fetch in fetches:
        fetch.start()
    for p in range(PANELS):
        for q in range(PANELS):
            part = diag_ref[:, q, p].reshape(TILE, TILE)
            work_ref[p * TILE : (p + 1) * TILE, q * TILE : (q + 1) * TILE] = part
    at_row = lax.broadcasted_iota(jnp.int32, (WIDTH, WIDTH), 0)
    at_col = lax.broadcasted_iota(jnp.int32, (WIDTH, WIDTH), 1)
    inverse_ref[...] = jnp.where(at_row == at_col, 1.0, 0.0).astype(jnp.float32)
    tile_rows = lower_ref.shape[0] // TILE
    sends = []
    order = [t % wraps * (tile_rows // wraps) + t // wraps for t in range(tile_rows)]
    for start in range(0, WIDTH, STRIP):
        stop = start + STRIP
        first = start // TILE * TILE
        upper = WIDTH - first
        done = first + TILE
        strip = jnp.concatenate(
            [work_ref[start:stop, first:], inverse_ref[start:stop, :done]], axis=1
        )
        strip = eliminate(strip, start - first)
        inverse_ref[start:stop, :done] = strip[:, upper:]
        if stop < WIDTH:
            update = product(strip[:, :upper], strip, ((0,), (0,)))[stop - first :]
            work_ref[stop:, first:] = work_ref[stop:, first:] - update[:, :upper]
            inverse_ref[stop:, :done] = inverse_ref[stop:, :done] - update[:, upper:]
        if stop % TILE == 0:
            if first == 0:
                for fetch in fetches:
                    fetch.wait()
            raw = jnp.concatenate(
                [
                    jnp.concatenate(
                        [raw_ref[p, :, at].reshape(TILE, TILE) for at in order], axis=0
                    )
                    for p in range(done // TILE)
                ],
                axis=1,
            )
            lower_ref[:, first:done] = product(raw, inverse_ref[first:done, :done], ((1,), (1,)))
            send = pltpu.make_async_copy(
                lower_ref.at[:, first:done], lower_hbm_ref.at[:, first:done], sems.at[first // TILE]
            )
            send.start()
            sends.append(send)
    for send in sends:
        send.wait()


def in_vmem(*arrays):
    return [pltpu.with_memory_space_constraint(x, pltpu.VMEM) for x in arrays]


def in_hbm(*arrays):
    return [pltpu.with_memory_space_constraint(x, pltpu.HBM) for x in arrays]


def panels(wraps, place, diag, own, other):
    count = own.shape[0] * own.shape[1] * GROUP
    hbm = pl.BlockSpec(memory_space=pltpu.HBM)
    vmem = pl.BlockSpec(memory_space=pltpu.VMEM)
    return pl.pallas_call(
        functools.partial(panels_kernel, wraps),
        out_shape=[
            pltpu.VMEM((WIDTH, WIDTH), jnp.float32),
            pltpu.HBM((count, WIDTH), jnp.float32),
        ],
        in_specs=[pl.BlockSpec(memory_space=pltpu.SMEM), vmem, hbm, hbm],
        out_specs=[vmem, hbm],
        scratch_shapes=[
            pltpu.VMEM((WIDTH, WIDTH), jnp.float32),
            pltpu.VMEM((PANELS, *own.shape), jnp.float32),
            pltpu.VMEM((count, WIDTH), jnp.float32),
            pltpu.SemaphoreType.DMA((2 * PANELS,)),
        ],
        cost_estimate=pl.CostEstimate(
            flops=4 * WIDTH**3 + 12 * count * WIDTH**2,
            bytes_accessed=12 * WIDTH**2 + 8 * count * WIDTH,
            transcendentals=0,
        ),
        compiler_params=pltpu.CompilerParams(vmem_limit_bytes=32 * 2**20),
        name="panels",
    )(place, *in_vmem(diag), *in_hbm(own, other))


def trailing_kernel(
    grid_rows, grid_cols, place_ref, matrix_ref, lower_hbm_ref, cols_ref, inverse_ref, out_ref, lower_ref, done_ref, sems
):
    fetch = pltpu.make_async_copy(lower_hbm_ref, lower_ref, sems.at[0])
    fetch.start()
    row_index, col_index = place_ref[0], place_ref[1]
    rows_count, cols_count = matrix_ref.shape
    tile_rows, tile_cols = rows_count // TILE, cols_count // TILE
    raw = jnp.concatenate(
        [
            jnp.concatenate(
                [
                    cols_ref[:, p, wrap, b].reshape(-1, TILE)
                    for b in range(tile_cols)
                    for wrap in range(cols_ref.shape[2])
                ],
                axis=0,
            )
            for p in range(PANELS)
        ],
        axis=1,
    )
    high, low = split(product(raw, inverse_ref[...], ((1,), (1,))))
    solved = jnp.concatenate([high, low, high], axis=1)
    fetch.wait()
    at_row = lax.broadcasted_iota(jnp.int32, (TILE, TILE), 0)
    at_col = lax.broadcasted_iota(jnp.int32, (TILE, TILE), 1)
    sends = []
    for step in reversed(range(tile_rows // STEP)):
        span = slice(step * STEP * TILE, (step + 1) * STEP * TILE)
        last_tile_row = ((step + 1) * STEP - 1) * grid_rows + grid_rows - 1
        reach = min(tile_cols, last_tile_row // grid_cols + 1)
        high, low = split(lower_ref[span, :])
        update = lax.dot_general(
            jnp.concatenate([high, high, low], axis=1),
            solved[: reach * TILE],
            (((1,), (1,)), ((), ())),
            preferred_element_type=jnp.float32,
        )
        for t in range(STEP):
            tile_row = (step * STEP + t) * grid_rows + row_index
            down = slice((step * STEP + t) * TILE, (step * STEP + t + 1) * TILE)
            for b in range(reach):
                across = slice(b * TILE, (b + 1) * TILE)
                tile_col = b * grid_cols + col_index
                value = matrix_ref[down, across] - update[t * TILE : (t + 1) * TILE, across]
                keep = tile_row >= tile_col
                if b * grid_cols < PANELS:
                    for p in range(PANELS):
                        panel = lower_ref[down, p * TILE : (p + 1) * TILE]
                        value = jnp.where(tile_col == p, panel, value)
                    inner = (tile_row - tile_col) * TILE + at_row - at_col >= 0
                    keep = inner | ((tile_row == tile_col) & (tile_col >= PANELS))
                done_ref[down, across] = jnp.where(keep, value, 0.0)
        if reach < tile_cols:
            beyond = slice(reach * TILE, cols_count)
            done_ref[span, beyond] = jnp.zeros((STEP * TILE, cols_count - reach * TILE), jnp.float32)
        send = pltpu.make_async_copy(done_ref.at[span], out_ref.at[span], sems.at[step + 1])
        send.start()
        sends.append(send)
    for send in sends:
        send.wait()


def trailing(grid_rows, grid_cols, place, matrix, lower, cols, inverse):
    vmem = pl.BlockSpec(memory_space=pltpu.VMEM)
    matrix, cols, inverse = in_vmem(matrix, cols, inverse)
    (lower,) = in_hbm(lower)
    return pl.pallas_call(
        functools.partial(trailing_kernel, grid_rows, grid_cols),
        out_shape=jax.ShapeDtypeStruct(matrix.shape, jnp.float32),
        in_specs=[
            pl.BlockSpec(memory_space=pltpu.SMEM),
            vmem,
            pl.BlockSpec(memory_space=pltpu.HBM),
            vmem,
            vmem,
        ],
        out_specs=pl.BlockSpec(memory_space=pl.ANY),
        scratch_shapes=[
            pltpu.VMEM(lower.shape, jnp.float32),
            pltpu.VMEM(matrix.shape, jnp.float32),
            pltpu.SemaphoreType.DMA((matrix.shape[0] // (STEP * TILE) + 1,)),
        ],
        compiler_params=pltpu.CompilerParams(vmem_limit_bytes=32 * 2**20),
        name="trailing",
    )(place, matrix, lower, cols, inverse)


def by_wrap_kernel(planes_ref, parts_ref, sems):
    copies = [
        pltpu.make_async_copy(planes_ref.at[:, w], parts_ref.at[w], sems.at[w])
        for w in range(parts_ref.shape[0])
    ]
    for copy in copies:
        copy.start()
    for copy in copies:
        copy.wait()


def by_wrap(planes):
    count, wraps, *rest = planes.shape
    return pl.pallas_call(
        by_wrap_kernel,
        out_shape=pltpu.HBM((wraps, count, *rest), planes.dtype),
        in_specs=[pl.BlockSpec(memory_space=pltpu.VMEM)],
        out_specs=pl.BlockSpec(memory_space=pltpu.HBM),
        scratch_shapes=[pltpu.SemaphoreType.DMA((wraps,))],
        cost_estimate=pl.CostEstimate(
            flops=0, bytes_accessed=8 * planes.size, transcendentals=0
        ),
        compiler_params=pltpu.CompilerParams(vmem_limit_bytes=2**20),
        name="by_wrap",
    )(*in_vmem(planes))


def first_tiles_kernel(matrix_ref, panel_ref, sems):
    tile_cols, wraps = matrix_ref.shape[:2]
    copies = []
    for w in range(wraps):
        for b in range(tile_cols):
            at = w * tile_cols + b
            source = matrix_ref.at[b, w, :, :, pl.ds(0, TILE)]
            copies.append(pltpu.make_async_copy(source, panel_ref.at[:, at], sems.at[at]))
    for copy in copies:
        copy.start()
    for copy in copies:
        copy.wait()


def first_tiles(matrix):
    tile_cols, wraps, chips, group, _ = matrix.shape
    return pl.pallas_call(
        first_tiles_kernel,
        out_shape=pltpu.VMEM((chips, wraps * tile_cols, group, TILE), matrix.dtype),
        in_specs=[pl.BlockSpec(memory_space=pltpu.HBM)],
        out_specs=pl.BlockSpec(memory_space=pltpu.VMEM),
        scratch_shapes=[pltpu.SemaphoreType.DMA((wraps * tile_cols,))],
        compiler_params=pltpu.CompilerParams(vmem_limit_bytes=2 * 2**20),
        name="first_tiles",
    )(*in_hbm(matrix))


def exchange(chunks, axis):
    return lax.all_to_all(chunks, axis, 0, 0, tiled=True)


def to_all(part, axis):
    count = lax.axis_size(axis)
    return exchange(jnp.broadcast_to(part[None], (count, *part.shape)), axis)


def on_device(matrix):
    rows_count, cols_count = matrix.shape
    grid_rows = lax.axis_size("row")
    grid_cols = lax.axis_size("col")
    chips = grid_cols // PANELS
    tile_cols = cols_count // TILE
    wraps = grid_cols // grid_rows
    place = jnp.stack([lax.axis_index("row"), lax.axis_index("col")]).astype(jnp.int32)
    with jax.named_scope("scatter_rows"):
        panel = first_tiles(matrix.reshape(tile_cols, wraps, chips, GROUP, cols_count))
        same_core = [list(range(p, grid_cols, PANELS)) for p in range(PANELS)]
        piece = lax.all_to_all(panel, "col", 0, 0, tiled=True, axis_index_groups=same_core)[0]
    with jax.named_scope("gather_rows"):
        copies = jnp.broadcast_to(piece[None], (chips, *piece.shape))
        own = lax.all_to_all(copies, "col", 0, 0, tiled=True, axis_index_groups=same_core)
    with jax.named_scope("gather_planes"):
        planes = lax.all_gather(piece, "row", tiled=True)
        own, planes = lax.optimization_barrier((own, planes))
        planes = planes.reshape(grid_rows, *piece.shape)
    with jax.named_scope("swap_panels"):
        other = lax.ppermute(own, "col", [(c, c ^ 1) for c in range(grid_cols)])
    with jax.named_scope("spread_diagonal"):
        diag = to_all(planes[:PANELS, 0], "col")
    with jax.named_scope("exchange_cols"):
        parts = by_wrap(planes.reshape(grid_rows, wraps, tile_cols, GROUP, TILE))
        diag, parts = lax.optimization_barrier((diag, parts))
        cols = exchange(parts.reshape(grid_cols, tile_cols, GROUP, TILE), "col")
        cols = cols.reshape(chips, PANELS, 1, *cols.shape[1:])
    diag = diag.reshape(chips, PANELS, *diag.shape[1:])
    inverse, lower = panels(wraps, place, diag, own, other)
    return trailing(grid_rows, grid_cols, place, matrix, lower, cols, inverse)


def solution(mesh):
    return jax.shard_map(
        on_device, mesh=mesh, in_specs=(P("row", "col"),), out_specs=P("row", "col"), check_vma=False
    )
```
